32 devices in a mesh: groups: 2 (over y), seq: 4 (over z), rep: 2 (over x), sub: 2 (over core).
Axes of the slice: x: 2, y: 2, z: 4, core: 2. Of those that a mesh axis runs over, the one named last changes fastest.
Arguments:
- queries: bfloat16 [4, 512, 32, 384], P(('groups', 'rep'), 'seq', None, 'sub'), parts along dimension 0, may hold values from -64 to 64
- grad_out: bfloat16 [4, 512, 32, 256], P(('groups', 'rep'), 'seq', None, 'sub'), parts along dimension 0, may hold values from -6 to 6
- latent_kv: bfloat16 [4, 512, 576], P(('groups', 'rep'), 'seq'), parts along dimension 0, may hold values from -24 to 24
- key_up: bfloat16 [32, 2, 128, 512], P('seq', 'sub'), may hold values from -0.25 to 0.25
- value_up: bfloat16 [32, 2, 512, 128], P('seq', 'sub'), may hold values from -0.25 to 0.25
- key_blocks: int32 [4, 4, 3], P(('groups', 'rep')), parts along dimension 0, may hold values from 0 to 3, as said below
- block_counts: int32 [4, 4], P(('groups', 'rep')), parts along dimension 0, may hold values from 1 to 3, as said below
Outputs:
- grad_queries: bfloat16 [4, 512, 32, 384], P(('groups', 'rep'), 'seq', None, 'sub'), parts along dimension 0
- grad_latent: float32 [4, 512, 576], P(('groups', 'rep'), 'seq', 'sub'), parts along dimension 0
- grad_key_up: float32 [64, 2, 128, 512], P(('groups', 'seq'), 'sub', 'rep'), parts along dimension 0
- grad_value_up: float32 [64, 2, 512, 128], P(('groups', 'seq'), 'sub', 'rep'), parts along dimension 0
The draws below stay inside these ranges and needn't reach their ends.
There are 2 independent parts, one for each index of `groups`. The reference program is written for one: setup_inputs(seed, part) draws one part's arguments, and reference() takes and returns one part's arrays. A program takes and returns all parts, laid end to end along the dimension named above; an argument that names none is the same for every part. Nothing has to cross between parts.
Inputs may be any that keep to these rules, and one draw needn't show every extreme that they name: `key_blocks`: row b of a sequence lists key blocks for query block b: its first entry is b, its first block_counts[b] entries are distinct and none exceeds b, and the remaining entries equal b. `block_counts`: query block b lists at most min(b + 1, 3) key blocks; the last query block of each sequence lists exactly 3.
All inputs are finite; a program needn't handle non-finite values.
Results may differ from the reference program's by a relative error of at most 0.012.
Values may be sent and summed in bfloat16 or wider, within the bound.
A program may use at most 128 MiB of HBM per device.

```python
import math
import jax
import jax.numpy as jnp
from jax import lax

NOPE = 128
VD = 128
LAT = 512
BLK = 128
MAXB = 3
HP = 32
QD = 192
KVW = 576
SEQS = 2
L = 512
NQB = 4


def latent_draw(key):
    folded = jax.random.fold_in(key, 101)
    key_one = jax.random.fold_in(folded, 0)
    values = jnp.clip(jax.random.normal(key_one, (SEQS, L, KVW), jnp.float32), -6.0, 6.0)
    return values


def draw_latent_kv(key, part):
    return latent_draw(key).astype(jnp.bfloat16)


def draw_queries(key, part):
    folded = jax.random.fold_in(key, 202)
    key_one = jax.random.fold_in(folded, 0)
    values = jnp.clip(jax.random.normal(key_one, (SEQS, L, HP, 2 * QD), jnp.float32), -6.0, 6.0)
    return values.astype(jnp.bfloat16)


def block_lists(key):
    folded = jax.random.fold_in(key, 303)
    key_one, key_two = jax.random.split(folded, 2)
    query_block = jnp.arange(NQB, dtype=jnp.int32)
    upper_bound = jnp.minimum(query_block + 1, MAXB)
    counts = jax.random.randint(key_one, (SEQS, NQB), 1, upper_bound[None, :] + 1)
    counts = jnp.where(query_block[None, :] == NQB - 1, MAXB, counts).astype(jnp.int32)
    random_ints = jax.random.randint(key_two, (SEQS, NQB, NQB), 0, 1 << 20)
    column = jnp.arange(NQB, dtype=jnp.int32)
    sort_keys = random_ints * NQB + column[None, None, :]
    sort_keys = jnp.where(column[None, None, :] < query_block[None, :, None], sort_keys, (1 << 30) + column[None, None, :])
    picked = jnp.argsort(sort_keys, axis=2)[:, :, :MAXB - 1].astype(jnp.int32)
    own_block = jnp.broadcast_to(query_block[None, :, None], (SEQS, NQB, 1))
    slot_list = jnp.concatenate([own_block, picked], axis=2)
    slot_index = jnp.arange(MAXB, dtype=jnp.int32)
    slot_list = jnp.where(slot_index[None, None, :] < counts[:, :, None], slot_list, query_block[None, :, None])
    return (slot_list.astype(jnp.int32), counts)


def draw_key_blocks(key, part):
    return block_lists(key)[0]


def draw_block_counts(key, part):
    return block_lists(key)[1]


def shard_levels(key, dims, cuts, least, high):
    level, own = 1.0, jax.random.fold_in(key, 6)
    for dim, parts in cuts:
        steps = jnp.exp(jax.random.uniform(jax.random.fold_in(own, dim), (parts,), jnp.float32, least / len(cuts), high / len(cuts)))
        level = level * jnp.repeat(steps, dims[dim] // parts).reshape([-1 if axis == dim else 1 for axis in range(len(dims))])
    return level


def scatter_about(stream_key, dims, spread, limit, shards=(), kind=jnp.bfloat16):
    drawn = spread * jax.random.normal(stream_key, dims, jnp.float32)
    if shards:
        drawn = drawn * shard_levels(stream_key, dims, shards, -0.22, 0.18)
    return jnp.clip(drawn, -limit, limit).astype(kind)


def setup_inputs(seed: int = 0, part: int = 0) -> dict:
    arg_keys = jax.random.split(jax.random.key(seed), 8)
    own_keys = jax.random.split(jax.random.fold_in(arg_keys[7], part), 8)
    return {
        "queries": draw_queries(jax.random.fold_in(jax.random.fold_in(arg_keys[7], part), 71), part),
        "grad_out": scatter_about(own_keys[1], (SEQS, L, HP, 2 * VD), 1.0, 6.0, ((0, 2), (1, 4), (3, 2))),
        "latent_kv": draw_latent_kv(jax.random.fold_in(jax.random.fold_in(arg_keys[7], part), 71), part),
        "key_up": scatter_about(arg_keys[3], (HP, 2, NOPE, LAT), LAT ** -0.5, 0.25, ((0, 4), (1, 2))),
        "value_up": scatter_about(arg_keys[4], (HP, 2, LAT, VD), LAT ** -0.5, 0.25, ((0, 4), (1, 2))),
        "key_blocks": draw_key_blocks(jax.random.fold_in(jax.random.fold_in(arg_keys[7], part), 71), part),
        "block_counts": draw_block_counts(jax.random.fold_in(jax.random.fold_in(arg_keys[7], part), 71), part),
    }


def head_backward(head_queries, head_grads, latent, key_weight, value_weight, slot_list, count_list, block_rows):
    length = head_queries.shape[0]
    latent_width = key_weight.shape[1]
    nope_width = key_weight.shape[0]
    query_width = head_queries.shape[1]
    value_width = head_grads.shape[1]
    block_count = length // block_rows
    slot_count = slot_list.shape[1]
    factor = 1.0 / math.sqrt(query_width)
    compressed = latent[:, :latent_width]
    key_nope = jnp.dot(compressed, key_weight.T, preferred_element_type=jnp.float32).astype(jnp.bfloat16)
    values = jnp.dot(compressed, value_weight, preferred_element_type=jnp.float32).astype(jnp.bfloat16)
    keys_all = jnp.concatenate([key_nope, latent[:, latent_width:]], axis=1)
    key_tiles = keys_all.reshape(block_count, block_rows, query_width)
    value_tiles = values.reshape(block_count, block_rows, value_width)
    causal = lax.broadcasted_iota(jnp.int32, (block_rows, block_rows), 0) >= lax.broadcasted_iota(jnp.int32, (block_rows, block_rows), 1)
    slot_range = jnp.arange(slot_count, dtype=jnp.int32)

    def one_block(carry, inputs):
        key_total, value_total = carry
        query_tile, grad_tile, block_slots, block_live, block_index = inputs
        keys_here = key_tiles[block_slots].reshape(slot_count * block_rows, query_width).astype(jnp.float32)
        values_here = value_tiles[block_slots].reshape(slot_count * block_rows, value_width).astype(jnp.float32)
        live = slot_range < block_live
        diagonal = block_slots == block_index
        allowed = live[None, :, None] & (jnp.logical_not(diagonal)[None, :, None] | causal[:, None, :])
        allowed = allowed.reshape(block_rows, slot_count * block_rows)
        query_wide = query_tile.astype(jnp.float32)
        grad_wide = grad_tile.astype(jnp.float32)
        scores = jnp.einsum('qd,kd->qk', query_wide, keys_here) * factor
        scores = jnp.where(allowed, scores, -1e+30)
        top_score = lax.optimization_barrier(jnp.max(scores, axis=1, keepdims=True))
        expo = jnp.where(allowed, jnp.exp(scores - top_score), 0.0)
        probs = expo / lax.optimization_barrier(jnp.sum(expo, axis=1, keepdims=True))
        probs_b = probs.astype(jnp.bfloat16)
        probs_wide = probs_b.astype(jnp.float32)
        attended = jnp.einsum('qk,kd->qd', probs_wide, values_here)
        delta = lax.optimization_barrier(jnp.sum(grad_wide * attended, axis=1, keepdims=True))
        grad_probs = jnp.einsum('qd,kd->qk', grad_wide, values_here)
        grad_scores = (probs * (grad_probs - delta)).astype(jnp.bfloat16).astype(jnp.float32)
        grad_query = (jnp.einsum('qk,kd->qd', grad_scores, keys_here) * factor).astype(jnp.bfloat16)
        grad_key = jnp.einsum('qk,qd->kd', grad_scores, query_wide) * factor
        grad_value = jnp.einsum('qk,qd->kd', probs_wide, grad_wide)
        key_total = key_total.at[block_slots].add(grad_key.reshape(slot_count, block_rows, query_width))
        value_total = value_total.at[block_slots].add(grad_value.reshape(slot_count, block_rows, value_width))
        return ((key_total, value_total), grad_query)
    start = (jnp.zeros((block_count, block_rows, query_width), jnp.float32), jnp.zeros((block_count, block_rows, value_width), jnp.float32))
    inputs = (head_queries.reshape(block_count, block_rows, query_width), head_grads.reshape(block_count, block_rows, value_width), slot_list, count_list, jnp.arange(block_count, dtype=jnp.int32))
    (key_total, value_total), grad_tiles = lax.scan(one_block, start, inputs)
    grad_query = grad_tiles.reshape(length, query_width)
    key_grads = key_total.reshape(length, query_width)
    nope_grads = key_grads[:, :nope_width].astype(jnp.bfloat16)
    value_grads = value_total.reshape(length, value_width).astype(jnp.bfloat16)
    latent_grad = jnp.dot(nope_grads, key_weight, preferred_element_type=jnp.float32) + jnp.dot(value_grads, value_weight.T, preferred_element_type=jnp.float32)
    head_part = jnp.concatenate([latent_grad, key_grads[:, nope_width:]], axis=1).astype(jnp.bfloat16)
    key_weight_grad = jnp.dot(nope_grads.T, compressed, preferred_element_type=jnp.float32)
    value_weight_grad = jnp.dot(compressed.T, value_grads, preferred_element_type=jnp.float32)
    return (grad_query, head_part, key_weight_grad, value_weight_grad)

def reference(queries, grad_out, latent_kv, key_up, value_up, key_blocks, block_counts):
    head_total = 2 * HP
    key_flat = key_up.reshape(head_total, NOPE, LAT)
    value_flat = value_up.reshape(head_total, LAT, VD)
    query_list = []
    latent_list = []
    key_sum = jnp.zeros((head_total, NOPE, LAT), jnp.float32)
    value_sum = jnp.zeros((head_total, LAT, VD), jnp.float32)
    for sequence in range(queries.shape[0]):
        query_heads = jnp.transpose(queries[sequence].reshape(L, head_total, QD), (1, 0, 2))
        grad_heads = jnp.transpose(grad_out[sequence].reshape(L, head_total, VD), (1, 0, 2))
        latent = latent_kv[sequence]
        slot_list = key_blocks[sequence]
        count_list = block_counts[sequence]

        def one_head(total, inputs):
            head_q, head_g, key_weight, value_weight = inputs
            grad_query, head_part, key_weight_grad, value_weight_grad = head_backward(head_q, head_g, latent, key_weight, value_weight, slot_list, count_list, BLK)
            return (total + head_part.astype(jnp.float32), (grad_query, key_weight_grad, value_weight_grad))
        latent_total, (query_grads, key_grads, value_grads) = lax.scan(one_head, jnp.zeros((L, KVW), jnp.float32), (query_heads, grad_heads, key_flat, value_flat))
        query_list.append(jnp.transpose(query_grads, (1, 0, 2)).reshape(L, HP, 2 * QD))
        latent_list.append(latent_total)
        key_sum = key_sum + key_grads
        value_sum = value_sum + value_grads
    return (jnp.stack(query_list), jnp.stack(latent_list), key_sum.reshape(HP, 2, NOPE, LAT), value_sum.reshape(HP, 2, LAT, VD))
```

```python
import functools
import math

import jax
import jax.numpy as jnp
from jax import lax
from jax.experimental import pallas as pl
from jax.experimental.pallas import tpu as pltpu
from jax.sharding import PartitionSpec as P

BLK = 128
NN = (((1,), (0,)), ((), ()))
NT = (((1,), (1,)), ((), ()))


def mm(a, b, dims=NN):
    return lax.dot_general(a, b, dims, preferred_element_type=jnp.float32)


def head_math(q_of, g_of, k_w, v_w, lat_t, lat, bias, keys, keys_t, dk, dv, blocks, store_dq):
    nope = k_w.shape[0]
    width = k_w.shape[1]
    total = lat_t.shape[1]
    query_width = keys_t.shape[0]
    factor = 1.0 / math.sqrt(query_width)
    keys[:, :nope] = mm(lat[:, :width], k_w, NT).astype(jnp.bfloat16)
    keys_t[:nope, :] = mm(k_w, lat_t[:width, :]).astype(jnp.bfloat16)
    values = mm(lat[:, :width], v_w).astype(jnp.bfloat16)
    for pair in reversed(range(blocks // 2)):
        seen = (2 * pair + 2) * BLK
        q2 = jnp.concatenate([q_of(2 * pair), q_of(2 * pair + 1)], axis=1)
        g2 = jnp.concatenate([g_of(2 * pair), g_of(2 * pair + 1)], axis=1)
        scores = mm(keys[:seen, :query_width], q2) * factor
        scores = scores + bias[:seen, 2 * pair * BLK : seen]
        expo = jnp.exp(scores - jnp.max(scores, axis=0, keepdims=True))
        probs = expo * (1.0 / jnp.sum(expo, axis=0, keepdims=True))
        probs_b = probs.astype(jnp.bfloat16)
        grad_probs = mm(values[:seen], g2)
        delta = jnp.sum(probs_b.astype(jnp.float32) * grad_probs, axis=0, keepdims=True)
        grad_scores = (probs * (grad_probs - delta)).astype(jnp.bfloat16)
        dq = (mm(keys_t[:, :seen], grad_scores) * factor).astype(jnp.bfloat16)
        store_dq(2 * pair, dq[:, :BLK])
        store_dq(2 * pair + 1, dq[:, BLK:])
        dk_part = mm(q2, grad_scores, NT)
        dv_part = mm(g2, probs_b, NT)
        if seen == total:
            dk[...] = dk_part
            dv[...] = dv_part
        else:
            dk[:, :seen] += dk_part
            dv[:, :seen] += dv_part
    nope_b = (dk[:nope, :] * factor).astype(jnp.bfloat16)
    rope = dk[nope:, :] * factor
    value_b = dv[...].astype(jnp.bfloat16)
    latent_part = mm(k_w.T, nope_b) + mm(v_w, value_b)
    k_grad = mm(nope_b, lat_t[:width, :], NT)
    v_grad = mm(lat_t[:width, :], value_b, NT)
    return latent_part, rope, k_grad, v_grad


def block_bias(slots, counts, blocks):
    live = jnp.arange(slots.shape[1], dtype=jnp.int32)[None, :] < counts[:, None]
    blocks_here = jnp.arange(blocks, dtype=jnp.int32)
    listed = jnp.any((slots[None] == blocks_here[:, None, None]) & live[None], axis=2)
    position = jnp.arange(blocks * BLK, dtype=jnp.int32)
    wide = jnp.repeat(jnp.repeat(listed, BLK, axis=0), BLK, axis=1)
    allowed = wide & (position[:, None] <= position[None, :])
    return jnp.where(allowed, 0.0, -1e30).astype(jnp.float32)


def attention_kernel(
    blocks, q_ref, g_ref, lat_t, bias, k_ref, v_ref, dq_ref, dlat_ref, dk_ref, dv_ref,
    lat, keys, keys_t, dk, dv
):
    width = k_ref.shape[2]
    nope = k_ref.shape[1]

    @pl.when(pl.program_id(0) == 0)
    def _():
        dlat_ref[...] = jnp.zeros_like(dlat_ref)
        lat[...] = lat_t[:width, :].T
        keys[:, nope : keys_t.shape[0]] = lat_t[width:, :].T
        keys_t[nope:, :] = lat_t[width:, :]

    def store_dq(block, value):
        dq_ref[block, 0] = value

    latent_part, rope, k_grad, v_grad = head_math(
        lambda b: q_ref[b, 0], lambda b: g_ref[b, 0], k_ref[0], v_ref[0], lat_t, lat, bias,
        keys, keys_t, dk, dv, blocks, store_dq
    )
    dlat_ref[:width, :] += latent_part
    dlat_ref[width:, :] += rope
    dk_ref[0] = k_grad
    dv_ref[0] = v_grad


def attention_call(q_all, g_all, lat_t, bias, k_w, v_w):
    blocks, heads, query_width, _ = q_all.shape
    value_width = g_all.shape[2]
    kv_width, total = lat_t.shape
    nope, width = k_w.shape[1:]
    whole = lambda *shape: pl.BlockSpec(shape, lambda h: (0,) * len(shape))
    return pl.pallas_call(
        functools.partial(attention_kernel, blocks),
        grid=(heads,),
        in_specs=[
            pl.BlockSpec((blocks, 1, query_width, BLK), lambda h: (0, h, 0, 0)),
            pl.BlockSpec((blocks, 1, value_width, BLK), lambda h: (0, h, 0, 0)),
            whole(kv_width, total),
            whole(total, total),
            pl.BlockSpec((1, nope, width), lambda h: (h, 0, 0)),
            pl.BlockSpec((1, width, value_width), lambda h: (h, 0, 0)),
        ],
        out_specs=[
            pl.BlockSpec((blocks, 1, query_width, BLK), lambda h: (0, h, 0, 0)),
            whole(kv_width, total),
            pl.BlockSpec((1, nope, width), lambda h: (h, 0, 0)),
            pl.BlockSpec((1, width, value_width), lambda h: (h, 0, 0)),
        ],
        out_shape=[
            jax.ShapeDtypeStruct(q_all.shape, jnp.bfloat16),
            jax.ShapeDtypeStruct((kv_width, total), jnp.float32),
            jax.ShapeDtypeStruct(k_w.shape, jnp.float32),
            jax.ShapeDtypeStruct(v_w.shape, jnp.float32),
        ],
        scratch_shapes=[
            pltpu.VMEM((total, width), jnp.bfloat16),
            pltpu.VMEM((total, 2 * BLK), jnp.bfloat16),
            pltpu.VMEM((query_width, total), jnp.bfloat16),
            pltpu.VMEM((query_width, total), jnp.float32),
            pltpu.VMEM((value_width, total), jnp.float32),
        ],
        compiler_params=pltpu.CompilerParams(
            dimension_semantics=("arbitrary",), vmem_limit_bytes=40 << 20
        ),
    )(q_all, g_all, lat_t, bias, k_w, v_w)


def halves_exchange(grads, dim):
    rows = grads.shape[dim] // 2
    index = lax.axis_index("rep")
    mine = lax.dynamic_slice_in_dim(grads, index * rows, rows, dim)
    other = lax.dynamic_slice_in_dim(grads, (1 - index) * rows, rows, dim).astype(jnp.bfloat16)
    return mine + lax.ppermute(other, "rep", [(0, 1), (1, 0)]).astype(jnp.float32)


def local_small(queries, grad_out, latent_kv, key_up, value_up, key_blocks, block_counts):
    shards = lax.axis_size("seq")
    heads = key_up.shape[0]
    tokens = queries.shape[1]
    q_t = jnp.transpose(queries[0], (1, 2, 0))
    g_t = jnp.transpose(grad_out[0], (1, 2, 0))
    lat_t = lax.all_gather(latent_kv[0].T, "seq", axis=1, tiled=True)
    q_all = lax.all_to_all(q_t, "seq", split_axis=0, concat_axis=0, tiled=True)
    g_all = lax.all_to_all(g_t, "seq", split_axis=0, concat_axis=0, tiled=True)
    q_all = q_all.reshape(shards, heads, q_t.shape[1], tokens)
    g_all = g_all.reshape(shards, heads, g_t.shape[1], tokens)
    bias = block_bias(key_blocks[0], block_counts[0], shards)
    dq, dlat, dk, dv = attention_call(
        q_all, g_all, lat_t, bias, key_up[:, 0], value_up[:, 0]
    )
    returned = lax.all_to_all(
        dq.reshape(shards * heads, q_t.shape[1], tokens), "seq", split_axis=0, concat_axis=0,
        tiled=True
    )
    grad_queries = jnp.transpose(returned, (2, 0, 1))[None]
    half = lax.psum_scatter(dlat, "sub", scatter_dimension=0, tiled=True)
    grad_latent = lax.psum_scatter(half, "seq", scatter_dimension=1, tiled=True)
    return (
        grad_queries,
        grad_latent.T[None],
        halves_exchange(dk[:, None], 2),
        halves_exchange(dv[:, None], 2),
    )


def head_backward(
    head_queries, head_grads, latent, key_weight, value_weight, slot_list, count_list, block_rows
):
    length = head_queries.shape[0]
    latent_width = key_weight.shape[1]
    nope_width = key_weight.shape[0]
    query_width = head_queries.shape[1]
    value_width = head_grads.shape[1]
    block_count = length // block_rows
    slot_count = slot_list.shape[1]
    factor = 1.0 / math.sqrt(query_width)
    compressed = latent[:, :latent_width]
    key_nope = jnp.einsum(
        "tl,dl->td", compressed, key_weight, preferred_element_type=jnp.float32
    ).astype(jnp.bfloat16)
    values = jnp.dot(compressed, value_weight, preferred_element_type=jnp.float32).astype(
        jnp.bfloat16
    )
    keys_all = jnp.concatenate([key_nope, latent[:, latent_width:]], axis=1)
    per_group = math.gcd(block_count, max(1, 512 // block_rows))
    group_count = block_count // per_group
    key_tiles = keys_all.reshape(block_count, block_rows, query_width)
    value_tiles = values.reshape(block_count, block_rows, value_width)
    causal = lax.broadcasted_iota(jnp.int32, (block_rows, block_rows), 0) >= lax.broadcasted_iota(
        jnp.int32, (block_rows, block_rows), 1
    )
    slot_range = jnp.arange(slot_count, dtype=jnp.int32)
    within = jnp.arange(per_group, dtype=jnp.int32)

    def one_group(carry, inputs):
        key_total, value_total = carry
        query_tile, grad_tile, group_slots, group_counts, group_index = inputs
        own_blocks = group_index * per_group + within
        keys_here = key_tiles[group_slots].reshape(per_group, slot_count * block_rows, query_width)
        values_here = value_tiles[group_slots].reshape(
            per_group, slot_count * block_rows, value_width
        )
        live = slot_range[None, :] < group_counts[:, None]
        diagonal = group_slots == own_blocks[:, None]
        allowed = live[:, None, :, None] & (
            jnp.logical_not(diagonal)[:, None, :, None] | causal[None, :, None, :]
        )
        allowed = allowed.reshape(per_group, block_rows, slot_count * block_rows)
        scores = (
            jnp.einsum("gqd,gkd->gqk", query_tile, keys_here, preferred_element_type=jnp.float32)
            * factor
        )
        scores = jnp.where(allowed, scores, -1e30)
        top_score = jnp.max(scores, axis=2, keepdims=True)
        expo = jnp.where(allowed, jnp.exp(scores - top_score), 0.0)
        probs = expo / jnp.sum(expo, axis=2, keepdims=True)
        probs_b = probs.astype(jnp.bfloat16)
        attended = jnp.einsum(
            "gqk,gkd->gqd", probs_b, values_here, preferred_element_type=jnp.float32
        )
        delta = jnp.sum(grad_tile.astype(jnp.float32) * attended, axis=2, keepdims=True)
        grad_probs = jnp.einsum(
            "gqd,gkd->gqk", grad_tile, values_here, preferred_element_type=jnp.float32
        )
        grad_scores = (probs * (grad_probs - delta)).astype(jnp.bfloat16)
        grad_query = (
            jnp.einsum("gqk,gkd->gqd", grad_scores, keys_here, preferred_element_type=jnp.float32)
            * factor
        ).astype(jnp.bfloat16)
        grad_key = (
            jnp.einsum("gqk,gqd->gkd", grad_scores, query_tile, preferred_element_type=jnp.float32)
            * factor
        )
        grad_value = jnp.einsum(
            "gqk,gqd->gkd", probs_b, grad_tile, preferred_element_type=jnp.float32
        )
        flat_slots = group_slots.reshape(per_group * slot_count)
        key_total = key_total.at[flat_slots].add(
            grad_key.reshape(per_group * slot_count, block_rows, query_width)
        )
        value_total = value_total.at[flat_slots].add(
            grad_value.reshape(per_group * slot_count, block_rows, value_width)
        )
        return ((key_total, value_total), grad_query)

    start = (
        jnp.zeros((block_count, block_rows, query_width), jnp.float32),
        jnp.zeros((block_count, block_rows, value_width), jnp.float32),
    )
    inputs = (
        head_queries.reshape(group_count, per_group, block_rows, query_width),
        head_grads.reshape(group_count, per_group, block_rows, value_width),
        slot_list.reshape(group_count, per_group, slot_count),
        count_list.reshape(group_count, per_group),
        jnp.arange(group_count, dtype=jnp.int32),
    )
    (key_total, value_total), grad_tiles = lax.scan(one_group, start, inputs)
    grad_query = grad_tiles.reshape(length, query_width)
    key_grads = key_total.reshape(length, query_width)
    nope_grads = key_grads[:, :nope_width].astype(jnp.bfloat16)
    value_grads = value_total.reshape(length, value_width).astype(jnp.bfloat16)
    latent_grad = jnp.dot(nope_grads, key_weight, preferred_element_type=jnp.float32) + jnp.einsum(
        "tv,lv->tl", value_grads, value_weight, preferred_element_type=jnp.float32
    )
    head_part = jnp.concatenate([latent_grad, key_grads[:, nope_width:]], axis=1).astype(
        jnp.bfloat16
    )
    key_weight_grad = jnp.einsum(
        "td,tl->dl", nope_grads, compressed, preferred_element_type=jnp.float32
    )
    value_weight_grad = jnp.einsum(
        "tl,tv->lv", compressed, value_grads, preferred_element_type=jnp.float32
    )
    return (grad_query, head_part, key_weight_grad, value_weight_grad)


def local_general(queries, grad_out, latent_kv, key_up, value_up, key_blocks, block_counts):
    head_queries, head_grads = (
        lax.all_to_all(queries, "seq", split_axis=2, concat_axis=1, tiled=True),
        lax.all_to_all(grad_out, "seq", split_axis=2, concat_axis=1, tiled=True),
    )
    latent = lax.all_gather(latent_kv, "seq", axis=1, tiled=True)[0]
    slot_list = key_blocks[0]
    count_list = block_counts[0]
    query_stack = jnp.moveaxis(head_queries[0], 1, 0)
    grad_stack = jnp.moveaxis(head_grads[0], 1, 0)

    def one_head(carry, inputs):
        head_q, head_g, key_weight, value_weight = inputs
        results = head_backward(
            head_q, head_g, latent, key_weight, value_weight, slot_list, count_list, BLK
        )
        return (carry, results)

    unused, (query_grads, head_parts, key_grads, value_grads) = lax.scan(
        one_head,
        jnp.zeros((), jnp.float32),
        (query_stack, grad_stack, key_up[:, 0], value_up[:, 0]),
    )
    returning = jnp.moveaxis(query_grads, 0, 1)[None]
    grad_queries = lax.all_to_all(returning, "seq", split_axis=1, concat_axis=2, tiled=True)
    heads_here, length, part_width = head_parts.shape
    seq_count = lax.axis_size("seq")
    tokens_here = length // seq_count
    pieces = head_parts.reshape(heads_here, seq_count, tokens_here, part_width)
    arrived = lax.all_to_all(pieces, "seq", split_axis=1, concat_axis=1, tiled=True)
    summed = jnp.sum(arrived.astype(jnp.float32), axis=(0, 1))
    grad_latent = lax.psum_scatter(summed, "sub", scatter_dimension=1, tiled=True)
    key_grads = key_grads[:, None]
    value_grads = value_grads[:, None]
    total_key, total_value = lax.psum((key_grads, value_grads), "rep")
    replica_count = lax.axis_size("rep")
    replica_index = lax.axis_index("rep")
    key_rows = total_key.shape[2] // replica_count
    value_rows = total_value.shape[2] // replica_count
    grad_key_up = lax.dynamic_slice_in_dim(total_key, replica_index * key_rows, key_rows, 2)
    grad_value_up = lax.dynamic_slice_in_dim(total_value, replica_index * value_rows, value_rows, 2)
    return (grad_queries, grad_latent[None], grad_key_up, grad_value_up)


def solution(mesh):
    placed = (
        P(("groups", "rep"), "seq", None, "sub"),
        P(("groups", "rep"), "seq", None, "sub"),
        P(("groups", "rep"), "seq", None),
        P("seq", "sub", None, None),
        P("seq", "sub", None, None),
        P(("groups", "rep"), None, None),
        P(("groups", "rep"), None),
    )

    def local(queries, grad_out, latent_kv, key_up, value_up, key_blocks, block_counts):
        args = (queries, grad_out, latent_kv, key_up, value_up, key_blocks, block_counts)
        shards = mesh.shape["seq"]
        small = (
            queries.shape[1] == BLK
            and shards % 2 == 0
            and shards * BLK <= 1024
            and mesh.shape["rep"] == 2
        )
        return local_small(*args) if small else local_general(*args)

    return jax.shard_map(
        local,
        mesh=mesh,
        in_specs=placed,
        out_specs=(
            P(("groups", "rep"), "seq", None, "sub"),
            P(("groups", "rep"), "seq", "sub"),
            P(("groups", "seq"), "sub", "rep", None),
            P(("groups", "seq"), "sub", "rep", None),
        ),
        check_vma=False,
    )
```

```python
import functools
import math

import jax
import jax.numpy as jnp
from jax import lax
from jax.experimental import pallas as pl
from jax.experimental.pallas import tpu as pltpu
from jax.sharding import PartitionSpec as P

BLK = 128
NN = (((1,), (0,)), ((), ()))
NT = (((1,), (1,)), ((), ()))


def mm(a, b, dims=NN):
    return lax.dot_general(a, b, dims, preferred_element_type=jnp.float32)


def head_math(q_of, g_of, k_w, v_w, lat_t, lat, bias, keys, keys_t, dk, dv, blocks, store_dq):
    nope = k_w.shape[0]
    width = k_w.shape[1]
    total = lat_t.shape[1]
    query_width = keys_t.shape[0]
    factor = 1.0 / math.sqrt(query_width)
    keys[:, :nope] = mm(lat[...], k_w, NT).astype(jnp.bfloat16)
    keys_t[:nope, :] = mm(k_w, lat_t[:width, :]).astype(jnp.bfloat16)
    values = mm(lat[...], v_w).astype(jnp.bfloat16)
    for pair in reversed(range(blocks // 2)):
        seen = (2 * pair + 2) * BLK
        q2 = jnp.concatenate([q_of(2 * pair), q_of(2 * pair + 1)], axis=1)
        g2 = jnp.concatenate([g_of(2 * pair), g_of(2 * pair + 1)], axis=0)
        scores = mm(keys[:seen, :query_width], q2) * factor
        scores = scores + bias[:seen, 2 * pair * BLK : seen]
        expo = jnp.exp(scores - jnp.max(scores, axis=0, keepdims=True))
        probs = expo * (1.0 / jnp.sum(expo, axis=0, keepdims=True))
        probs_b = probs.astype(jnp.bfloat16)
        grad_probs = mm(values[:seen], g2, NT)
        delta = jnp.sum(probs_b.astype(jnp.float32) * grad_probs, axis=0, keepdims=True)
        grad_scores = (probs * (grad_probs - delta)).astype(jnp.bfloat16)
        dq = (mm(keys_t[:, :seen], grad_scores) * factor).astype(jnp.bfloat16)
        store_dq(2 * pair, dq[:, :BLK])
        store_dq(2 * pair + 1, dq[:, BLK:])
        dk_part = mm(q2, grad_scores, NT)
        dv_part = mm(probs_b, g2)
        if seen == total:
            dk[...] = dk_part
            dv[...] = dv_part
        else:
            dk[:, :seen] += dk_part
            dv[:seen, :] += dv_part
    nope_b = (dk[:nope, :] * factor).astype(jnp.bfloat16)
    rope = dk[nope:, :] * factor
    value_b = dv[...].astype(jnp.bfloat16)
    latent_part = mm(k_w.T, nope_b) + mm(v_w, value_b, NT)
    k_grad = mm(nope_b, lat_t[:width, :], NT)
    v_grad = mm(lat_t[:width, :], value_b)
    return latent_part, rope, k_grad, v_grad


AHEAD = 4


def attention_kernel(
    shards, heads,
    slots, counts, q_in, g_in, lat_in, k_in, v_in,
    dq_out, lat_out, dk_out, dv_out,
    q_buf, g_buf, lat_buf, k_w, v_w, dq_buf, lat_t, lat, bias, keys, keys_t, dk, dv, dlat,
    k_half, v_half, kx_out, kx_in, vx_out, vx_in, half_in, piece_out, piece_in,
    q_send, q_recv, g_send, g_recv, lat_send, lat_recv, dq_send, dq_recv, dq_local,
    kx_sem, vx_sem, half_sem, piece_send, piece_recv, own_sem,
):
    me = lax.axis_index("seq")
    rep = lax.axis_index("rep")
    sub = lax.axis_index("sub")
    kv_width, total = lat_t.shape
    width = lat.shape[1]
    nope = k_w.shape[1]
    query_width = keys_t.shape[0]
    k_rows = kx_in.shape[1]
    v_rows = vx_in.shape[1]
    half_rows = kv_width // 2
    peers = range(1, shards)

    def peer(d):
        return lax.rem(me + d, shards)

    def remote(src, dst, send, recv, axis, index):
        return pltpu.make_async_remote_copy(
            src_ref=src, dst_ref=dst, send_sem=send, recv_sem=recv,
            device_id={axis: index}, device_id_type=pl.DeviceIdType.MESH,
        )

    def q_copy(d, h):
        return remote(q_in.at[peer(d) * heads + h], q_buf.at[me, h],
                      q_send.at[d - 1, h], q_recv.at[d - 1, h], "seq", peer(d))

    def g_copy(d, h):
        return remote(g_in.at[peer(d) * heads + h], g_buf.at[me, h],
                      g_send.at[d - 1, h], g_recv.at[d - 1, h], "seq", peer(d))

    def lat_copy(d):
        return remote(lat_in, lat_buf.at[me], lat_send.at[d - 1], lat_recv.at[d - 1],
                      "seq", peer(d))

    def dq_copy(d, h):
        return remote(dq_buf.at[peer(d), h], dq_out.at[me * heads + h],
                      dq_send.at[d - 1, h], dq_recv.at[d - 1, h], "seq", peer(d))

    def dq_own(h):
        return pltpu.make_async_copy(
            dq_buf.at[me, h], dq_out.at[me * heads + h], dq_local.at[h])

    def k_copy(h):
        return remote(kx_out.at[h], kx_in.at[h], kx_sem.at[0, h], kx_sem.at[1, h],
                      "rep", 1 - rep)

    def v_copy(h):
        return remote(vx_out.at[h], vx_in.at[h], vx_sem.at[0, h], vx_sem.at[1, h],
                      "rep", 1 - rep)

    barrier = pltpu.get_barrier_semaphore()
    for d in peers:
        pl.semaphore_signal(barrier, inc=1, device_id={"seq": peer(d)},
                            device_id_type=pl.DeviceIdType.MESH)
    pl.semaphore_signal(barrier, inc=1, device_id={"rep": 1 - rep},
                        device_id_type=pl.DeviceIdType.MESH)
    pl.semaphore_signal(barrier, inc=1, device_id={"sub": 1 - sub},
                        device_id_type=pl.DeviceIdType.MESH)
    pl.semaphore_wait(barrier, shards + 1)

    for d in peers:
        lat_copy(d).start()

    def send_head(h):
        for d in peers:
            q_copy(d, h).start()
            g_copy(d, h).start()

    def first(h, unused):
        send_head(h)
        return unused

    lax.fori_loop(0, min(AHEAD, heads), first, 0)
    own = pl.ds(me * heads, heads)
    locals_ = [
        pltpu.make_async_copy(lat_in, lat_buf.at[me], own_sem.at[0]),
        pltpu.make_async_copy(q_in.at[own], q_buf.at[me], own_sem.at[1]),
        pltpu.make_async_copy(g_in.at[own], g_buf.at[me], own_sem.at[2]),
        pltpu.make_async_copy(k_in, k_w, own_sem.at[3]),
        pltpu.make_async_copy(v_in, v_w, own_sem.at[4]),
    ]
    for copy in locals_:
        copy.start()

    causal = lax.broadcasted_iota(jnp.int32, (BLK, BLK), 0) <= lax.broadcasted_iota(
        jnp.int32, (BLK, BLK), 1
    )
    for key_block in range(shards):
        for query_block in range(shards):
            hit = jnp.int32(0)
            for m in range(slots.shape[1]):
                same = (slots[query_block, m] == key_block) & (m < counts[query_block])
                hit = hit | same.astype(jnp.int32)
            if key_block > query_block:
                hit = jnp.int32(0)
            wide = jnp.full((BLK, BLK), hit, jnp.int32) > 0
            if key_block == query_block:
                wide = wide & causal
            bias[key_block * BLK : (key_block + 1) * BLK,
                 query_block * BLK : (query_block + 1) * BLK] = jnp.where(
                     wide, 0.0, -1e30).astype(jnp.float32)
    dlat[...] = jnp.zeros_like(dlat)
    for copy in locals_:
        copy.wait()
    for d in peers:
        lat_copy(d).wait()
    for b in range(shards):
        columns = slice(b * BLK, (b + 1) * BLK)
        lat_t[:, columns] = lat_buf[b]
        lat[columns, :] = lat_buf[b, :width, :].T
        keys[columns, nope:query_width] = lat_buf[b, width:, :].T
        keys_t[nope:, columns] = lat_buf[b, width:, :]

    def one_head(h, unused):
        @pl.when(h + AHEAD < heads)
        def _():
            send_head(h + AHEAD)

        for d in peers:
            q_copy(d, h).wait()
            g_copy(d, h).wait()

        def store_dq(block, value):
            dq_buf[block, h] = value

        latent_part, rope, k_grad, v_grad = head_math(
            lambda b: q_buf[b, h], lambda b: g_buf[b, h], k_w[h], v_w[h], lat_t, lat, bias,
            keys, keys_t, dk, dv, shards, store_dq
        )
        for d in peers:
            dq_copy(d, h).start()
        dq_own(h).start()
        dlat[:width, :] += latent_part
        dlat[width:, :] += rope
        k_half[...] = k_grad
        v_half[...] = v_grad
        kx_out[h] = k_half[pl.ds((1 - rep) * k_rows, k_rows), :].astype(jnp.bfloat16)
        vx_out[h] = v_half[pl.ds((1 - rep) * v_rows, v_rows), :].astype(jnp.bfloat16)
        k_copy(h).start()
        v_copy(h).start()
        dk_out[h] = k_half[pl.ds(rep * k_rows, k_rows), :]
        dv_out[h] = v_half[pl.ds(rep * v_rows, v_rows), :]
        return unused

    lax.fori_loop(0, heads, one_head, 0)

    exchange = remote(dlat.at[pl.ds((1 - sub) * half_rows, half_rows), :], half_in,
                      half_sem.at[0], half_sem.at[1], "sub", 1 - sub)
    exchange.start()

    def finish(h, unused):
        k_copy(h).wait()
        v_copy(h).wait()
        dk_out[h] += kx_in[h].astype(jnp.float32)
        dv_out[h] += vx_in[h].astype(jnp.float32)
        return unused

    exchange.wait()
    half_in[...] += dlat[pl.ds(sub * half_rows, half_rows), :]
    for b in range(shards):
        piece_out[b] = half_in[:, b * BLK : (b + 1) * BLK].astype(jnp.bfloat16)

    def piece_copy(d):
        return remote(piece_out.at[peer(d)], piece_in.at[d - 1],
                      piece_send.at[d - 1], piece_recv.at[d - 1], "seq", peer(d))

    for d in peers:
        piece_copy(d).start()
    lax.fori_loop(0, heads, finish, 0)
    gathered = half_in[:, pl.ds(pl.multiple_of(me * BLK, BLK), BLK)]
    for d in peers:
        piece_copy(d).wait()
        gathered = gathered + piece_in[d - 1].astype(jnp.float32)
    lat_out[...] = gathered

    def drain(h, unused):
        for d in peers:
            dq_copy(d, h).wait()
        dq_own(h).wait()
        return unused

    lax.fori_loop(0, heads, drain, 0)


def local_small(queries, grad_out, latent_kv, key_up, value_up, key_blocks, block_counts):
    shards = lax.axis_size("seq")
    heads, _, nope, width = key_up.shape
    value_width = value_up.shape[3]
    q_t = jnp.transpose(queries[0], (1, 2, 0))
    g_t = jnp.transpose(grad_out[0], (1, 0, 2))
    lat_local = latent_kv[0].T
    kv_width, tokens = lat_local.shape
    total = shards * tokens
    query_width = q_t.shape[1]
    half = kv_width // 2
    bf16, f32 = jnp.bfloat16, jnp.float32
    hbm = pl.BlockSpec(memory_space=pl.ANY)
    vmem = pl.BlockSpec(memory_space=pltpu.VMEM)
    smem = pl.BlockSpec(memory_space=pltpu.SMEM)
    sems = lambda *shape: pltpu.SemaphoreType.DMA(shape)
    far = shards - 1
    dq, dlat, dk, dv = pl.pallas_call(
        functools.partial(attention_kernel, shards, heads),
        in_specs=[smem, smem, hbm, hbm, hbm, hbm, hbm],
        out_specs=[hbm, vmem, vmem, vmem],
        out_shape=[
            jax.ShapeDtypeStruct(q_t.shape, bf16),
            jax.ShapeDtypeStruct((half, tokens), f32),
            jax.ShapeDtypeStruct((heads, nope // 2, width), f32),
            jax.ShapeDtypeStruct((heads, width // 2, value_width), f32),
        ],
        scratch_shapes=[
            pltpu.VMEM((shards, heads, query_width, tokens), bf16),
            pltpu.VMEM((shards, heads, tokens, value_width), bf16),
            pltpu.VMEM((shards, kv_width, tokens), bf16),
            pltpu.VMEM((heads, nope, width), bf16),
            pltpu.VMEM((heads, width, value_width), bf16),
            pltpu.VMEM((shards, heads, query_width, tokens), bf16),
            pltpu.VMEM((kv_width, total), bf16),
            pltpu.VMEM((total, width), bf16),
            pltpu.VMEM((total, total), f32),
            pltpu.VMEM((total, 2 * BLK), bf16),
            pltpu.VMEM((query_width, total), bf16),
            pltpu.VMEM((query_width, total), f32),
            pltpu.VMEM((total, value_width), f32),
            pltpu.VMEM((kv_width, total), f32),
            pltpu.VMEM((nope, width), f32),
            pltpu.VMEM((width, value_width), f32),
            pltpu.VMEM((heads, nope // 2, width), bf16),
            pltpu.VMEM((heads, nope // 2, width), bf16),
            pltpu.VMEM((heads, width // 2, value_width), bf16),
            pltpu.VMEM((heads, width // 2, value_width), bf16),
            pltpu.VMEM((half, total), f32),
            pltpu.VMEM((shards, half, tokens), bf16),
            pltpu.VMEM((far, half, tokens), bf16),
            sems(far, heads), sems(far, heads), sems(far, heads), sems(far, heads),
            sems(far), sems(far),
            sems(far, heads), sems(far, heads), sems(heads),
            sems(2, heads), sems(2, heads), sems(2), sems(far), sems(far), sems(5),
        ],
        compiler_params=pltpu.CompilerParams(
            collective_id=0, has_side_effects=True, vmem_limit_bytes=48 << 20
        ),
    )(key_blocks[0], block_counts[0], q_t, g_t, lat_local, key_up[:, 0], value_up[:, 0])
    return (
        jnp.transpose(dq, (2, 0, 1))[None],
        dlat.T[None],
        dk[:, None],
        dv[:, None],
    )


def head_backward(
    head_queries, head_grads, latent, key_weight, value_weight, slot_list, count_list, block_rows
):
    length = head_queries.shape[0]
    latent_width = key_weight.shape[1]
    nope_width = key_weight.shape[0]
    query_width = head_queries.shape[1]
    value_width = head_grads.shape[1]
    block_count = length // block_rows
    slot_count = slot_list.shape[1]
    factor = 1.0 / math.sqrt(query_width)
    compressed = latent[:, :latent_width]
    key_nope = jnp.einsum(
        "tl,dl->td", compressed, key_weight, preferred_element_type=jnp.float32
    ).astype(jnp.bfloat16)
    values = jnp.dot(compressed, value_weight, preferred_element_type=jnp.float32).astype(
        jnp.bfloat16
    )
    keys_all = jnp.concatenate([key_nope, latent[:, latent_width:]], axis=1)
    per_group = math.gcd(block_count, max(1, 512 // block_rows))
    group_count = block_count // per_group
    key_tiles = keys_all.reshape(block_count, block_rows, query_width)
    value_tiles = values.reshape(block_count, block_rows, value_width)
    causal = lax.broadcasted_iota(jnp.int32, (block_rows, block_rows), 0) >= lax.broadcasted_iota(
        jnp.int32, (block_rows, block_rows), 1
    )
    slot_range = jnp.arange(slot_count, dtype=jnp.int32)
    within = jnp.arange(per_group, dtype=jnp.int32)

    def one_group(carry, inputs):
        key_total, value_total = carry
        query_tile, grad_tile, group_slots, group_counts, group_index = inputs
        own_blocks = group_index * per_group + within
        keys_here = key_tiles[group_slots].reshape(per_group, slot_count * block_rows, query_width)
        values_here = value_tiles[group_slots].reshape(
            per_group, slot_count * block_rows, value_width
        )
        live = slot_range[None, :] < group_counts[:, None]
        diagonal = group_slots == own_blocks[:, None]
        allowed = live[:, None, :, None] & (
            jnp.logical_not(diagonal)[:, None, :, None] | causal[None, :, None, :]
        )
        allowed = allowed.reshape(per_group, block_rows, slot_count * block_rows)
        scores = (
            jnp.einsum("gqd,gkd->gqk", query_tile, keys_here, preferred_element_type=jnp.float32)
            * factor
        )
        scores = jnp.where(allowed, scores, -1e30)
        top_score = jnp.max(scores, axis=2, keepdims=True)
        expo = jnp.where(allowed, jnp.exp(scores - top_score), 0.0)
        probs = expo / jnp.sum(expo, axis=2, keepdims=True)
        probs_b = probs.astype(jnp.bfloat16)
        attended = jnp.einsum(
            "gqk,gkd->gqd", probs_b, values_here, preferred_element_type=jnp.float32
        )
        delta = jnp.sum(grad_tile.astype(jnp.float32) * attended, axis=2, keepdims=True)
        grad_probs = jnp.einsum(
            "gqd,gkd->gqk", grad_tile, values_here, preferred_element_type=jnp.float32
        )
        grad_scores = (probs * (grad_probs - delta)).astype(jnp.bfloat16)
        grad_query = (
            jnp.einsum("gqk,gkd->gqd", grad_scores, keys_here, preferred_element_type=jnp.float32)
            * factor
        ).astype(jnp.bfloat16)
        grad_key = (
            jnp.einsum("gqk,gqd->gkd", grad_scores, query_tile, preferred_element_type=jnp.float32)
            * factor
        )
        grad_value = jnp.einsum(
            "gqk,gqd->gkd", probs_b, grad_tile, preferred_element_type=jnp.float32
        )
        flat_slots = group_slots.reshape(per_group * slot_count)
        key_total = key_total.at[flat_slots].add(
            grad_key.reshape(per_group * slot_count, block_rows, query_width)
        )
        value_total = value_total.at[flat_slots].add(
            grad_value.reshape(per_group * slot_count, block_rows, value_width)
        )
        return ((key_total, value_total), grad_query)

    start = (
        jnp.zeros((block_count, block_rows, query_width), jnp.float32),
        jnp.zeros((block_count, block_rows, value_width), jnp.float32),
    )
    inputs = (
        head_queries.reshape(group_count, per_group, block_rows, query_width),
        head_grads.reshape(group_count, per_group, block_rows, value_width),
        slot_list.reshape(group_count, per_group, slot_count),
        count_list.reshape(group_count, per_group),
        jnp.arange(group_count, dtype=jnp.int32),
    )
    (key_total, value_total), grad_tiles = lax.scan(one_group, start, inputs)
    grad_query = grad_tiles.reshape(length, query_width)
    key_grads = key_total.reshape(length, query_width)
    nope_grads = key_grads[:, :nope_width].astype(jnp.bfloat16)
    value_grads = value_total.reshape(length, value_width).astype(jnp.bfloat16)
    latent_grad = jnp.dot(nope_grads, key_weight, preferred_element_type=jnp.float32) + jnp.einsum(
        "tv,lv->tl", value_grads, value_weight, preferred_element_type=jnp.float32
    )
    head_part = jnp.concatenate([latent_grad, key_grads[:, nope_width:]], axis=1).astype(
        jnp.bfloat16
    )
    key_weight_grad = jnp.einsum(
        "td,tl->dl", nope_grads, compressed, preferred_element_type=jnp.float32
    )
    value_weight_grad = jnp.einsum(
        "tl,tv->lv", compressed, value_grads, preferred_element_type=jnp.float32
    )
    return (grad_query, head_part, key_weight_grad, value_weight_grad)


def local_general(queries, grad_out, latent_kv, key_up, value_up, key_blocks, block_counts):
    head_queries, head_grads = (
        lax.all_to_all(queries, "seq", split_axis=2, concat_axis=1, tiled=True),
        lax.all_to_all(grad_out, "seq", split_axis=2, concat_axis=1, tiled=True),
    )
    latent = lax.all_gather(latent_kv, "seq", axis=1, tiled=True)[0]
    slot_list = key_blocks[0]
    count_list = block_counts[0]
    query_stack = jnp.moveaxis(head_queries[0], 1, 0)
    grad_stack = jnp.moveaxis(head_grads[0], 1, 0)

    def one_head(carry, inputs):
        head_q, head_g, key_weight, value_weight = inputs
        results = head_backward(
            head_q, head_g, latent, key_weight, value_weight, slot_list, count_list, BLK
        )
        return (carry, results)

    unused, (query_grads, head_parts, key_grads, value_grads) = lax.scan(
        one_head,
        jnp.zeros((), jnp.float32),
        (query_stack, grad_stack, key_up[:, 0], value_up[:, 0]),
    )
    returning = jnp.moveaxis(query_grads, 0, 1)[None]
    grad_queries = lax.all_to_all(returning, "seq", split_axis=1, concat_axis=2, tiled=True)
    heads_here, length, part_width = head_parts.shape
    seq_count = lax.axis_size("seq")
    tokens_here = length // seq_count
    pieces = head_parts.reshape(heads_here, seq_count, tokens_here, part_width)
    arrived = lax.all_to_all(pieces, "seq", split_axis=1, concat_axis=1, tiled=True)
    summed = jnp.sum(arrived.astype(jnp.float32), axis=(0, 1))
    grad_latent = lax.psum_scatter(summed, "sub", scatter_dimension=1, tiled=True)
    key_grads = key_grads[:, None]
    value_grads = value_grads[:, None]
    total_key, total_value = lax.psum((key_grads, value_grads), "rep")
    replica_count = lax.axis_size("rep")
    replica_index = lax.axis_index("rep")
    key_rows = total_key.shape[2] // replica_count
    value_rows = total_value.shape[2] // replica_count
    grad_key_up = lax.dynamic_slice_in_dim(total_key, replica_index * key_rows, key_rows, 2)
    grad_value_up = lax.dynamic_slice_in_dim(total_value, replica_index * value_rows, value_rows, 2)
    return (grad_queries, grad_latent[None], grad_key_up, grad_value_up)


def solution(mesh):
    placed = (
        P(("groups", "rep"), "seq", None, "sub"),
        P(("groups", "rep"), "seq", None, "sub"),
        P(("groups", "rep"), "seq", None),
        P("seq", "sub", None, None),
        P("seq", "sub", None, None),
        P(("groups", "rep"), None, None),
        P(("groups", "rep"), None),
    )

    def local(queries, grad_out, latent_kv, key_up, value_up, key_blocks, block_counts):
        args = (queries, grad_out, latent_kv, key_up, value_up, key_blocks, block_counts)
        shards = mesh.shape["seq"]
        small = (
            queries.shape[1] == BLK
            and shards % 2 == 0
            and shards * BLK <= 1024
            and mesh.shape["rep"] == 2
            and mesh.shape["sub"] == 2
        )
        return local_small(*args) if small else local_general(*args)

    return jax.shard_map(
        local,
        mesh=mesh,
        in_specs=placed,
        out_specs=(
            P(("groups", "rep"), "seq", None, "sub"),
            P(("groups", "rep"), "seq", "sub"),
            P(("groups", "seq"), "sub", "rep", None),
            P(("groups", "seq"), "sub", "rep", None),
        ),
        check_vma=False,
    )
```

```python
import functools
import math

import jax
import jax.numpy as jnp
from jax import lax
from jax.experimental import pallas as pl
from jax.experimental.pallas import tpu as pltpu
from jax.sharding import PartitionSpec as P

BLK = 128
NN = (((1,), (0,)), ((), ()))
NT = (((1,), (1,)), ((), ()))


def mm(a, b, dims=NN):
    return lax.dot_general(a, b, dims, preferred_element_type=jnp.float32)


def head_math(q_of, g_of, k_w, v_w, lat_t, lat, bias, keys, keys_t, dk, dv, blocks, store_dq):
    nope = k_w.shape[0]
    width = k_w.shape[1]
    total = lat_t.shape[1]
    query_width = keys_t.shape[0]
    factor = 1.0 / math.sqrt(query_width)
    keys[:, :nope] = mm(lat[...], k_w, NT).astype(jnp.bfloat16)
    keys_t[:nope, :] = mm(k_w, lat_t[:width, :]).astype(jnp.bfloat16)
    values = mm(lat[...], v_w).astype(jnp.bfloat16)
    for pair in reversed(range(blocks // 2)):
        seen = (2 * pair + 2) * BLK
        q2 = jnp.concatenate([q_of(2 * pair), q_of(2 * pair + 1)], axis=1)
        g2 = jnp.concatenate([g_of(2 * pair), g_of(2 * pair + 1)], axis=0)
        scores = mm(keys[:seen, :query_width], q2) * factor
        scores = scores + bias[:seen, 2 * pair * BLK : seen]
        expo = jnp.exp(scores - jnp.max(scores, axis=0, keepdims=True))
        probs = expo * (1.0 / jnp.sum(expo, axis=0, keepdims=True))
        probs_b = probs.astype(jnp.bfloat16)
        grad_probs = mm(values[:seen], g2, NT)
        delta = jnp.sum(probs_b.astype(jnp.float32) * grad_probs, axis=0, keepdims=True)
        grad_scores = (probs * (grad_probs - delta)).astype(jnp.bfloat16)
        dq = (mm(keys_t[:, :seen], grad_scores) * factor).astype(jnp.bfloat16)
        store_dq(2 * pair, dq[:, :BLK])
        store_dq(2 * pair + 1, dq[:, BLK:])
        dk_part = mm(q2, grad_scores, NT)
        dv_part = mm(probs_b, g2)
        if seen == total:
            dk[...] = dk_part
            dv[...] = dv_part
        else:
            dk[:, :seen] += dk_part
            dv[:seen, :] += dv_part
    nope_b = (dk[:nope, :] * factor).astype(jnp.bfloat16)
    rope = dk[nope:, :] * factor
    value_b = dv[...].astype(jnp.bfloat16)
    latent_part = mm(k_w.T, nope_b) + mm(v_w, value_b, NT)
    k_grad = mm(nope_b, lat_t[:width, :], NT)
    v_grad = mm(lat_t[:width, :], value_b)
    return latent_part, rope, k_grad, v_grad


AHEAD = 4


def attention_kernel(
    shards, heads,
    slots, counts, q_in, g_in, lat_in, k_in, v_in,
    dq_out, lat_out, dk_out, dv_out,
    q_buf, g_buf, lat_buf, k_w, v_w, dq_buf, lat_t, lat, bias, keys, keys_t, dk, dv, dlat,
    k_half, v_half, kx_out, kx_in, vx_out, vx_in, half_in, piece_out, piece_in, cross_out, cross_in,
    q_send, q_recv, g_send, g_recv, lat_send, lat_recv, dq_send, dq_recv, dq_local,
    kx_sem, vx_sem, half_sem, piece_send, piece_recv, own_sem,
    share_send, share_recv,
):
    me = lax.axis_index("seq")
    rep = lax.axis_index("rep")
    sub = lax.axis_index("sub")
    kv_width, total = lat_t.shape
    width = lat.shape[1]
    nope = k_w.shape[1]
    query_width = keys_t.shape[0]
    k_rows = kx_in.shape[1]
    v_rows = vx_in.shape[1]
    half_rows = kv_width // 2
    peers = range(1, shards)
    lat_rows = pl.ds(pl.multiple_of(sub * half_rows, 16), half_rows)

    def peer(d):
        return lax.rem(me + d, shards)

    def remote(src, dst, send, recv, axis, index):
        return pltpu.make_async_remote_copy(
            src_ref=src, dst_ref=dst, send_sem=send, recv_sem=recv,
            device_id={axis: index}, device_id_type=pl.DeviceIdType.MESH,
        )

    def q_copy(d, h):
        return remote(q_in.at[peer(d) * heads + h], q_buf.at[me, h],
                      q_send.at[d - 1, h], q_recv.at[d - 1, h], "seq", peer(d))

    def g_copy(d, h):
        return remote(g_in.at[peer(d) * heads + h], g_buf.at[me, h],
                      g_send.at[d - 1, h], g_recv.at[d - 1, h], "seq", peer(d))

    near = me + 1 - 2 * lax.rem(me, 2)
    cross = lax.rem(me + 2, 4)
    diagonal = 3 - me

    def lat_copy(slot, src, source, target):
        return remote(src, lat_buf.at[source, lat_rows],
                      lat_send.at[slot], lat_recv.at[slot], "seq", target)

    lat_near = lat_copy(0, lat_in.at[lat_rows], me, near)
    lat_cross = lat_copy(1, lat_in.at[lat_rows], me, cross)
    lat_relay = lat_copy(2, lat_buf.at[cross, lat_rows], cross, near)

    def share_copy(slot, source):
        return remote(lat_buf.at[source, lat_rows], lat_buf.at[source, lat_rows],
                      share_send.at[slot], share_recv.at[slot], "sub", 1 - sub)

    def dq_copy(d, h):
        return remote(dq_buf.at[peer(d), h], dq_out.at[me * heads + h],
                      dq_send.at[d - 1, h], dq_recv.at[d - 1, h], "seq", peer(d))

    def dq_own(h):
        return pltpu.make_async_copy(
            dq_buf.at[me, h], dq_out.at[me * heads + h], dq_local.at[h])

    def k_copy(h):
        return remote(kx_out.at[h], kx_in.at[h], kx_sem.at[0, h], kx_sem.at[1, h],
                      "rep", 1 - rep)

    def v_copy(h):
        return remote(vx_out.at[h], vx_in.at[h], vx_sem.at[0, h], vx_sem.at[1, h],
                      "rep", 1 - rep)

    barrier = pltpu.get_barrier_semaphore()
    for d in peers:
        pl.semaphore_signal(barrier, inc=1, device_id={"seq": peer(d)},
                            device_id_type=pl.DeviceIdType.MESH)
    pl.semaphore_signal(barrier, inc=1, device_id={"rep": 1 - rep},
                        device_id_type=pl.DeviceIdType.MESH)
    pl.semaphore_signal(barrier, inc=1, device_id={"sub": 1 - sub},
                        device_id_type=pl.DeviceIdType.MESH)
    pl.semaphore_wait(barrier, shards + 1)

    lat_cross.start()
    lat_near.start()

    def send_head(h):
        for d in peers:
            q_copy(d, h).start()
            g_copy(d, h).start()

    def first(h, unused):
        send_head(h)
        return unused

    lax.fori_loop(0, min(AHEAD, heads), first, 0)
    own = pl.ds(me * heads, heads)
    locals_ = [
        pltpu.make_async_copy(lat_in, lat_buf.at[me], own_sem.at[0]),
        pltpu.make_async_copy(q_in.at[own], q_buf.at[me], own_sem.at[1]),
        pltpu.make_async_copy(g_in.at[own], g_buf.at[me], own_sem.at[2]),
        pltpu.make_async_copy(k_in, k_w, own_sem.at[3]),
        pltpu.make_async_copy(v_in, v_w, own_sem.at[4]),
    ]
    for copy in locals_:
        copy.start()

    causal = lax.broadcasted_iota(jnp.int32, (BLK, BLK), 0) <= lax.broadcasted_iota(
        jnp.int32, (BLK, BLK), 1
    )
    for key_block in range(shards):
        for query_block in range(shards):
            hit = jnp.int32(0)
            for m in range(slots.shape[1]):
                same = (slots[query_block, m] == key_block) & (m < counts[query_block])
                hit = hit | same.astype(jnp.int32)
            if key_block > query_block:
                hit = jnp.int32(0)
            wide = jnp.full((BLK, BLK), hit, jnp.int32) > 0
            if key_block == query_block:
                wide = wide & causal
            bias[key_block * BLK : (key_block + 1) * BLK,
                 query_block * BLK : (query_block + 1) * BLK] = jnp.where(
                     wide, 0.0, -1e30).astype(jnp.float32)
    dlat[...] = jnp.zeros_like(dlat)
    for copy in locals_:
        copy.wait()
    shares = [share_copy(0, near), share_copy(1, cross), share_copy(2, diagonal)]
    lat_cross.wait()
    lat_relay.start()
    shares[1].start()
    lat_near.wait()
    shares[0].start()
    lat_relay.wait()
    shares[2].start()
    for copy in shares:
        copy.wait()
    for b in range(shards):
        columns = slice(b * BLK, (b + 1) * BLK)
        lat_t[:, columns] = lat_buf[b]
        lat[columns, :] = lat_buf[b, :width, :].T
        keys[columns, nope:query_width] = lat_buf[b, width:, :].T
        keys_t[nope:, columns] = lat_buf[b, width:, :]

    def one_head(h, unused):
        @pl.when(h + AHEAD < heads)
        def _():
            send_head(h + AHEAD)

        for d in peers:
            q_copy(d, h).wait()
            g_copy(d, h).wait()

        def store_dq(block, value):
            dq_buf[block, h] = value

        latent_part, rope, k_grad, v_grad = head_math(
            lambda b: q_buf[b, h], lambda b: g_buf[b, h], k_w[h], v_w[h], lat_t, lat, bias,
            keys, keys_t, dk, dv, shards, store_dq
        )
        for d in peers:
            dq_copy(d, h).start()
        dq_own(h).start()
        dlat[:width, :] += latent_part
        dlat[width:, :] += rope
        k_half[...] = k_grad
        v_half[...] = v_grad
        kx_out[h] = k_half[pl.ds((1 - rep) * k_rows, k_rows), :].astype(jnp.bfloat16)
        vx_out[h] = v_half[pl.ds((1 - rep) * v_rows, v_rows), :].astype(jnp.bfloat16)
        k_copy(h).start()
        v_copy(h).start()
        dk_out[h] = k_half[pl.ds(rep * k_rows, k_rows), :]
        dv_out[h] = v_half[pl.ds(rep * v_rows, v_rows), :]
        return unused

    lax.fori_loop(0, heads, one_head, 0)

    exchange = remote(dlat.at[pl.ds((1 - sub) * half_rows, half_rows), :], half_in,
                      half_sem.at[0], half_sem.at[1], "sub", 1 - sub)
    exchange.start()

    def finish(h, unused):
        k_copy(h).wait()
        v_copy(h).wait()
        dk_out[h] += kx_in[h].astype(jnp.float32)
        dv_out[h] += vx_in[h].astype(jnp.float32)
        return unused

    exchange.wait()
    half_in[...] += dlat[pl.ds(sub * half_rows, half_rows), :]

    def columns_of(block):
        return half_in[:, pl.ds(pl.multiple_of(block * BLK, BLK), BLK)]

    piece_out[0] = columns_of(near).astype(jnp.bfloat16)
    piece_out[1] = columns_of(diagonal).astype(jnp.bfloat16)
    beside = remote(piece_out, piece_in, piece_send.at[0], piece_recv.at[0], "seq", near)
    beside.start()
    beside.wait()
    cross_out[...] = (columns_of(cross) + piece_in[1].astype(jnp.float32)).astype(jnp.bfloat16)
    over = remote(cross_out, cross_in, piece_send.at[1], piece_recv.at[1], "seq", cross)
    over.start()
    lax.fori_loop(0, heads, finish, 0)
    gathered = columns_of(me) + piece_in[0].astype(jnp.float32)
    over.wait()
    lat_out[...] = gathered + cross_in[...].astype(jnp.float32)

    def drain(h, unused):
        for d in peers:
            dq_copy(d, h).wait()
        dq_own(h).wait()
        return unused

    lax.fori_loop(0, heads, drain, 0)


def local_small(queries, grad_out, latent_kv, key_up, value_up, key_blocks, block_counts):
    shards = lax.axis_size("seq")
    heads, _, nope, width = key_up.shape
    value_width = value_up.shape[3]
    q_t = jnp.transpose(queries[0], (1, 2, 0))
    g_t = jnp.transpose(grad_out[0], (1, 0, 2))
    lat_local = latent_kv[0].T
    kv_width, tokens = lat_local.shape
    total = shards * tokens
    query_width = q_t.shape[1]
    half = kv_width // 2
    bf16, f32 = jnp.bfloat16, jnp.float32
    hbm = pl.BlockSpec(memory_space=pl.ANY)
    vmem = pl.BlockSpec(memory_space=pltpu.VMEM)
    smem = pl.BlockSpec(memory_space=pltpu.SMEM)
    sems = lambda *shape: pltpu.SemaphoreType.DMA(shape)
    far = shards - 1
    dq, dlat, dk, dv = pl.pallas_call(
        functools.partial(attention_kernel, shards, heads),
        in_specs=[smem, smem, hbm, hbm, hbm, hbm, hbm],
        out_specs=[hbm, vmem, vmem, vmem],
        out_shape=[
            jax.ShapeDtypeStruct(q_t.shape, bf16),
            jax.ShapeDtypeStruct((half, tokens), f32),
            jax.ShapeDtypeStruct((heads, nope // 2, width), f32),
            jax.ShapeDtypeStruct((heads, width // 2, value_width), f32),
        ],
        scratch_shapes=[
            pltpu.VMEM((shards, heads, query_width, tokens), bf16),
            pltpu.VMEM((shards, heads, tokens, value_width), bf16),
            pltpu.VMEM((shards, kv_width, tokens), bf16),
            pltpu.VMEM((heads, nope, width), bf16),
            pltpu.VMEM((heads, width, value_width), bf16),
            pltpu.VMEM((shards, heads, query_width, tokens), bf16),
            pltpu.VMEM((kv_width, total), bf16),
            pltpu.VMEM((total, width), bf16),
            pltpu.VMEM((total, total), f32),
            pltpu.VMEM((total, 2 * BLK), bf16),
            pltpu.VMEM((query_width, total), bf16),
            pltpu.VMEM((query_width, total), f32),
            pltpu.VMEM((total, value_width), f32),
            pltpu.VMEM((kv_width, total), f32),
            pltpu.VMEM((nope, width), f32),
            pltpu.VMEM((width, value_width), f32),
            pltpu.VMEM((heads, nope // 2, width), bf16),
            pltpu.VMEM((heads, nope // 2, width), bf16),
            pltpu.VMEM((heads, width // 2, value_width), bf16),
            pltpu.VMEM((heads, width // 2, value_width), bf16),
            pltpu.VMEM((half, total), f32),
            pltpu.VMEM((2, half, tokens), bf16),
            pltpu.VMEM((2, half, tokens), bf16),
            pltpu.VMEM((half, tokens), bf16),
            pltpu.VMEM((half, tokens), bf16),
            sems(far, heads), sems(far, heads), sems(far, heads), sems(far, heads),
            sems(far), sems(far),
            sems(far, heads), sems(far, heads), sems(heads),
            sems(2, heads), sems(2, heads), sems(2), sems(2), sems(2), sems(5),
            sems(far), sems(far),
        ],
        compiler_params=pltpu.CompilerParams(
            collective_id=0, has_side_effects=True, vmem_limit_bytes=48 << 20
        ),
    )(key_blocks[0], block_counts[0], q_t, g_t, lat_local, key_up[:, 0], value_up[:, 0])
    return (
        jnp.transpose(dq, (2, 0, 1))[None],
        dlat.T[None],
        dk[:, None],
        dv[:, None],
    )


def head_backward(
    head_queries, head_grads, latent, key_weight, value_weight, slot_list, count_list, block_rows
):
    length = head_queries.shape[0]
    latent_width = key_weight.shape[1]
    nope_width = key_weight.shape[0]
    query_width = head_queries.shape[1]
    value_width = head_grads.shape[1]
    block_count = length // block_rows
    slot_count = slot_list.shape[1]
    factor = 1.0 / math.sqrt(query_width)
    compressed = latent[:, :latent_width]
    key_nope = jnp.einsum(
        "tl,dl->td", compressed, key_weight, preferred_element_type=jnp.float32
    ).astype(jnp.bfloat16)
    values = jnp.dot(compressed, value_weight, preferred_element_type=jnp.float32).astype(
        jnp.bfloat16
    )
    keys_all = jnp.concatenate([key_nope, latent[:, latent_width:]], axis=1)
    per_group = math.gcd(block_count, max(1, 512 // block_rows))
    group_count = block_count // per_group
    key_tiles = keys_all.reshape(block_count, block_rows, query_width)
    value_tiles = values.reshape(block_count, block_rows, value_width)
    causal = lax.broadcasted_iota(jnp.int32, (block_rows, block_rows), 0) >= lax.broadcasted_iota(
        jnp.int32, (block_rows, block_rows), 1
    )
    slot_range = jnp.arange(slot_count, dtype=jnp.int32)
    within = jnp.arange(per_group, dtype=jnp.int32)

    def one_group(carry, inputs):
        key_total, value_total = carry
        query_tile, grad_tile, group_slots, group_counts, group_index = inputs
        own_blocks = group_index * per_group + within
        keys_here = key_tiles[group_slots].reshape(per_group, slot_count * block_rows, query_width)
        values_here = value_tiles[group_slots].reshape(
            per_group, slot_count * block_rows, value_width
        )
        live = slot_range[None, :] < group_counts[:, None]
        diagonal = group_slots == own_blocks[:, None]
        allowed = live[:, None, :, None] & (
            jnp.logical_not(diagonal)[:, None, :, None] | causal[None, :, None, :]
        )
        allowed = allowed.reshape(per_group, block_rows, slot_count * block_rows)
        scores = (
            jnp.einsum("gqd,gkd->gqk", query_tile, keys_here, preferred_element_type=jnp.float32)
            * factor
        )
        scores = jnp.where(allowed, scores, -1e30)
        top_score = jnp.max(scores, axis=2, keepdims=True)
        expo = jnp.where(allowed, jnp.exp(scores - top_score), 0.0)
        probs = expo / jnp.sum(expo, axis=2, keepdims=True)
        probs_b = probs.astype(jnp.bfloat16)
        attended = jnp.einsum(
            "gqk,gkd->gqd", probs_b, values_here, preferred_element_type=jnp.float32
        )
        delta = jnp.sum(grad_tile.astype(jnp.float32) * attended, axis=2, keepdims=True)
        grad_probs = jnp.einsum(
            "gqd,gkd->gqk", grad_tile, values_here, preferred_element_type=jnp.float32
        )
        grad_scores = (probs * (grad_probs - delta)).astype(jnp.bfloat16)
        grad_query = (
            jnp.einsum("gqk,gkd->gqd", grad_scores, keys_here, preferred_element_type=jnp.float32)
            * factor
        ).astype(jnp.bfloat16)
        grad_key = (
            jnp.einsum("gqk,gqd->gkd", grad_scores, query_tile, preferred_element_type=jnp.float32)
            * factor
        )
        grad_value = jnp.einsum(
            "gqk,gqd->gkd", probs_b, grad_tile, preferred_element_type=jnp.float32
        )
        flat_slots = group_slots.reshape(per_group * slot_count)
        key_total = key_total.at[flat_slots].add(
            grad_key.reshape(per_group * slot_count, block_rows, query_width)
        )
        value_total = value_total.at[flat_slots].add(
            grad_value.reshape(per_group * slot_count, block_rows, value_width)
        )
        return ((key_total, value_total), grad_query)

    start = (
        jnp.zeros((block_count, block_rows, query_width), jnp.float32),
        jnp.zeros((block_count, block_rows, value_width), jnp.float32),
    )
    inputs = (
        head_queries.reshape(group_count, per_group, block_rows, query_width),
        head_grads.reshape(group_count, per_group, block_rows, value_width),
        slot_list.reshape(group_count, per_group, slot_count),
        count_list.reshape(group_count, per_group),
        jnp.arange(group_count, dtype=jnp.int32),
    )
    (key_total, value_total), grad_tiles = lax.scan(one_group, start, inputs)
    grad_query = grad_tiles.reshape(length, query_width)
    key_grads = key_total.reshape(length, query_width)
    nope_grads = key_grads[:, :nope_width].astype(jnp.bfloat16)
    value_grads = value_total.reshape(length, value_width).astype(jnp.bfloat16)
    latent_grad = jnp.dot(nope_grads, key_weight, preferred_element_type=jnp.float32) + jnp.einsum(
        "tv,lv->tl", value_grads, value_weight, preferred_element_type=jnp.float32
    )
    head_part = jnp.concatenate([latent_grad, key_grads[:, nope_width:]], axis=1).astype(
        jnp.bfloat16
    )
    key_weight_grad = jnp.einsum(
        "td,tl->dl", nope_grads, compressed, preferred_element_type=jnp.float32
    )
    value_weight_grad = jnp.einsum(
        "tl,tv->lv", compressed, value_grads, preferred_element_type=jnp.float32
    )
    return (grad_query, head_part, key_weight_grad, value_weight_grad)


def local_general(queries, grad_out, latent_kv, key_up, value_up, key_blocks, block_counts):
    head_queries, head_grads = (
        lax.all_to_all(queries, "seq", split_axis=2, concat_axis=1, tiled=True),
        lax.all_to_all(grad_out, "seq", split_axis=2, concat_axis=1, tiled=True),
    )
    latent = lax.all_gather(latent_kv, "seq", axis=1, tiled=True)[0]
    slot_list = key_blocks[0]
    count_list = block_counts[0]
    query_stack = jnp.moveaxis(head_queries[0], 1, 0)
    grad_stack = jnp.moveaxis(head_grads[0], 1, 0)

    def one_head(carry, inputs):
        head_q, head_g, key_weight, value_weight = inputs
        results = head_backward(
            head_q, head_g, latent, key_weight, value_weight, slot_list, count_list, BLK
        )
        return (carry, results)

    unused, (query_grads, head_parts, key_grads, value_grads) = lax.scan(
        one_head,
        jnp.zeros((), jnp.float32),
        (query_stack, grad_stack, key_up[:, 0], value_up[:, 0]),
    )
    returning = jnp.moveaxis(query_grads, 0, 1)[None]
    grad_queries = lax.all_to_all(returning, "seq", split_axis=1, concat_axis=2, tiled=True)
    heads_here, length, part_width = head_parts.shape
    seq_count = lax.axis_size("seq")
    tokens_here = length // seq_count
    pieces = head_parts.reshape(heads_here, seq_count, tokens_here, part_width)
    arrived = lax.all_to_all(pieces, "seq", split_axis=1, concat_axis=1, tiled=True)
    summed = jnp.sum(arrived.astype(jnp.float32), axis=(0, 1))
    grad_latent = lax.psum_scatter(summed, "sub", scatter_dimension=1, tiled=True)
    key_grads = key_grads[:, None]
    value_grads = value_grads[:, None]
    total_key, total_value = lax.psum((key_grads, value_grads), "rep")
    replica_count = lax.axis_size("rep")
    replica_index = lax.axis_index("rep")
    key_rows = total_key.shape[2] // replica_count
    value_rows = total_value.shape[2] // replica_count
    grad_key_up = lax.dynamic_slice_in_dim(total_key, replica_index * key_rows, key_rows, 2)
    grad_value_up = lax.dynamic_slice_in_dim(total_value, replica_index * value_rows, value_rows, 2)
    return (grad_queries, grad_latent[None], grad_key_up, grad_value_up)


def solution(mesh):
    placed = (
        P(("groups", "rep"), "seq", None, "sub"),
        P(("groups", "rep"), "seq", None, "sub"),
        P(("groups", "rep"), "seq", None),
        P("seq", "sub", None, None),
        P("seq", "sub", None, None),
        P(("groups", "rep"), None, None),
        P(("groups", "rep"), None),
    )

    def local(queries, grad_out, latent_kv, key_up, value_up, key_blocks, block_counts):
        args = (queries, grad_out, latent_kv, key_up, value_up, key_blocks, block_counts)
        shards = mesh.shape["seq"]
        small = (
            queries.shape[1] == BLK
            and shards == 4
            and mesh.shape["rep"] == 2
            and mesh.shape["sub"] == 2
            and latent_kv.shape[2] % 32 == 0
        )
        return local_small(*args) if small else local_general(*args)

    return jax.shard_map(
        local,
        mesh=mesh,
        in_specs=placed,
        out_specs=(
            P(("groups", "rep"), "seq", None, "sub"),
            P(("groups", "rep"), "seq", "sub"),
            P(("groups", "seq"), "sub", "rep", None),
            P(("groups", "seq"), "sub", "rep", None),
        ),
        check_vma=False,
    )
```

```python
import functools
import math

import jax
import jax.numpy as jnp
from jax import lax
from jax.experimental import pallas as pl
from jax.experimental.pallas import tpu as pltpu
from jax.sharding import PartitionSpec as P

BLK = 128
NN = (((1,), (0,)), ((), ()))
NT = (((1,), (1,)), ((), ()))


def mm(a, b, dims=NN):
    return lax.dot_general(a, b, dims, preferred_element_type=jnp.float32)


def head_math(q_of, g_of, k_w, v_w, lat_t, lat, bias, keys, keys_t, dk, dv, blocks, store_dq):
    nope = k_w.shape[0]
    width = k_w.shape[1]
    total = lat_t.shape[1]
    query_width = keys_t.shape[0]
    factor = 1.0 / math.sqrt(query_width)
    keys[:, :nope] = mm(lat[...], k_w, NT).astype(jnp.bfloat16)
    keys_t[:nope, :] = mm(k_w, lat_t[:width, :]).astype(jnp.bfloat16)
    values = mm(lat[...], v_w).astype(jnp.bfloat16)
    for pair in reversed(range(blocks // 2)):
        seen = (2 * pair + 2) * BLK
        q2 = jnp.concatenate([q_of(2 * pair), q_of(2 * pair + 1)], axis=1)
        g2 = jnp.concatenate([g_of(2 * pair), g_of(2 * pair + 1)], axis=0)
        scores = mm(keys[:seen, :query_width], q2) * factor
        scores = scores + bias[:seen, 2 * pair * BLK : seen]
        expo = jnp.exp(scores - jnp.max(scores, axis=0, keepdims=True))
        probs = expo * (1.0 / jnp.sum(expo, axis=0, keepdims=True))
        probs_b = probs.astype(jnp.bfloat16)
        grad_probs = mm(values[:seen], g2, NT)
        delta = jnp.sum(probs_b.astype(jnp.float32) * grad_probs, axis=0, keepdims=True)
        grad_scores = (probs * (grad_probs - delta)).astype(jnp.bfloat16)
        dq = (mm(keys_t[:, :seen], grad_scores) * factor).astype(jnp.bfloat16)
        store_dq(2 * pair, dq[:, :BLK])
        store_dq(2 * pair + 1, dq[:, BLK:])
        dk_part = mm(q2, grad_scores, NT)
        dv_part = mm(probs_b, g2)
        if seen == total:
            dk[...] = dk_part
            dv[...] = dv_part
        else:
            dk[:, :seen] += dk_part
            dv[:seen, :] += dv_part
    nope_b = (dk[:nope, :] * factor).astype(jnp.bfloat16)
    rope = dk[nope:, :] * factor
    value_b = dv[...].astype(jnp.bfloat16)
    latent_part = mm(k_w.T, nope_b) + mm(v_w, value_b, NT)
    k_grad = mm(nope_b, lat_t[:width, :], NT)
    v_grad = mm(lat_t[:width, :], value_b)
    return latent_part, rope, k_grad, v_grad


AHEAD = 8


def attention_kernel(
    shards, heads,
    slots, counts, q_in, g_in, lat_in, k_in, v_in,
    dq_out, lat_out, dk_out, dv_out,
    q_buf, g_buf, lat_buf, k_w, v_w, dq_buf, lat_t, lat, bias, keys, keys_t, dk, dv, dlat,
    k_half, v_half, kx_out, kx_in, vx_out, vx_in, half_in, piece_out, piece_in, cross_out, cross_in,
    q_send, q_recv, g_send, g_recv, lat_send, lat_recv, dq_send, dq_recv, dq_local,
    kx_sem, vx_sem, half_sem, piece_send, piece_recv, own_sem,
    share_send, share_recv,
):
    me = lax.axis_index("seq")
    rep = lax.axis_index("rep")
    sub = lax.axis_index("sub")
    kv_width, total = lat_t.shape
    width = lat.shape[1]
    nope = k_w.shape[1]
    query_width = keys_t.shape[0]
    k_rows = kx_in.shape[1]
    v_rows = vx_in.shape[1]
    half_rows = kv_width // 2
    peers = range(1, shards)
    lat_rows = pl.ds(pl.multiple_of(sub * half_rows, 16), half_rows)

    def peer(d):
        return (lax.rem(me + 2, 4), 3 - me, me + 1 - 2 * lax.rem(me, 2))[d - 1]

    def remote(src, dst, send, recv, axis, index):
        return pltpu.make_async_remote_copy(
            src_ref=src, dst_ref=dst, send_sem=send, recv_sem=recv,
            device_id={axis: index}, device_id_type=pl.DeviceIdType.MESH,
        )

    def q_copy(d, h):
        return remote(q_in.at[peer(d) * heads + h], q_buf.at[me, h],
                      q_send.at[d - 1, h], q_recv.at[d - 1, h], "seq", peer(d))

    def g_copy(d, h):
        return remote(g_in.at[peer(d) * heads + h], g_buf.at[me, h],
                      g_send.at[d - 1, h], g_recv.at[d - 1, h], "seq", peer(d))

    near = me + 1 - 2 * lax.rem(me, 2)
    cross = lax.rem(me + 2, 4)
    diagonal = 3 - me

    def lat_copy(slot, src, source, target):
        return remote(src, lat_buf.at[source, lat_rows],
                      lat_send.at[slot], lat_recv.at[slot], "seq", target)

    lat_near = lat_copy(0, lat_in.at[lat_rows], me, near)
    lat_cross = lat_copy(1, lat_in.at[lat_rows], me, cross)
    lat_relay = lat_copy(2, lat_buf.at[cross, lat_rows], cross, near)

    def share_copy(slot, source):
        return remote(lat_buf.at[source, lat_rows], lat_buf.at[source, lat_rows],
                      share_send.at[slot], share_recv.at[slot], "sub", 1 - sub)

    def dq_copy(d, h):
        return remote(dq_buf.at[peer(d), h], dq_out.at[me * heads + h],
                      dq_send.at[d - 1, h], dq_recv.at[d - 1, h], "seq", peer(d))

    def dq_own(h):
        return pltpu.make_async_copy(
            dq_buf.at[me, h], dq_out.at[me * heads + h], dq_local.at[h])

    def k_copy(h):
        return remote(kx_out.at[h], kx_in.at[h], kx_sem.at[0, h], kx_sem.at[1, h],
                      "rep", 1 - rep)

    def v_copy(h):
        return remote(vx_out.at[h], vx_in.at[h], vx_sem.at[0, h], vx_sem.at[1, h],
                      "rep", 1 - rep)

    barrier = pltpu.get_barrier_semaphore()
    for d in peers:
        pl.semaphore_signal(barrier, inc=1, device_id={"seq": peer(d)},
                            device_id_type=pl.DeviceIdType.MESH)
    pl.semaphore_signal(barrier, inc=1, device_id={"rep": 1 - rep},
                        device_id_type=pl.DeviceIdType.MESH)
    pl.semaphore_signal(barrier, inc=1, device_id={"sub": 1 - sub},
                        device_id_type=pl.DeviceIdType.MESH)
    pl.semaphore_wait(barrier, shards + 1)

    lat_cross.start()
    lat_near.start()

    def send_head(h):
        for d in peers:
            q_copy(d, h).start()
            g_copy(d, h).start()

    def first(h, unused):
        send_head(h)
        return unused

    lax.fori_loop(0, min(AHEAD, heads), first, 0)
    own = pl.ds(me * heads, heads)
    locals_ = [
        pltpu.make_async_copy(lat_in, lat_buf.at[me], own_sem.at[0]),
        pltpu.make_async_copy(q_in.at[own], q_buf.at[me], own_sem.at[1]),
        pltpu.make_async_copy(g_in.at[own], g_buf.at[me], own_sem.at[2]),
        pltpu.make_async_copy(k_in, k_w, own_sem.at[3]),
        pltpu.make_async_copy(v_in, v_w, own_sem.at[4]),
    ]
    for copy in locals_:
        copy.start()

    causal = lax.broadcasted_iota(jnp.int32, (BLK, BLK), 0) <= lax.broadcasted_iota(
        jnp.int32, (BLK, BLK), 1
    )
    for key_block in range(shards):
        for query_block in range(shards):
            hit = jnp.int32(0)
            for m in range(slots.shape[1]):
                same = (slots[query_block, m] == key_block) & (m < counts[query_block])
                hit = hit | same.astype(jnp.int32)
            if key_block > query_block:
                hit = jnp.int32(0)
            wide = jnp.full((BLK, BLK), hit, jnp.int32) > 0
            if key_block == query_block:
                wide = wide & causal
            bias[key_block * BLK : (key_block + 1) * BLK,
                 query_block * BLK : (query_block + 1) * BLK] = jnp.where(
                     wide, 0.0, -1e30).astype(jnp.float32)
    dlat[...] = jnp.zeros_like(dlat)
    for copy in locals_:
        copy.wait()
    shares = [share_copy(0, near), share_copy(1, cross), share_copy(2, diagonal)]
    lat_cross.wait()
    lat_relay.start()
    shares[1].start()
    lat_near.wait()
    shares[0].start()
    lat_relay.wait()
    shares[2].start()
    for copy in shares:
        copy.wait()
    for b in range(shards):
        columns = slice(b * BLK, (b + 1) * BLK)
        lat_t[:, columns] = lat_buf[b]
        lat[columns, :] = lat_buf[b, :width, :].T
        keys[columns, nope:query_width] = lat_buf[b, width:, :].T
        keys_t[nope:, columns] = lat_buf[b, width:, :]

    def one_head(h, unused):
        @pl.when(h + AHEAD < heads)
        def _():
            send_head(h + AHEAD)

        for d in peers:
            q_copy(d, h).wait()
            g_copy(d, h).wait()

        def store_dq(block, value):
            dq_buf[block, h] = value

        latent_part, rope, k_grad, v_grad = head_math(
            lambda b: q_buf[b, h], lambda b: g_buf[b, h], k_w[h], v_w[h], lat_t, lat, bias,
            keys, keys_t, dk, dv, shards, store_dq
        )
        for d in peers:
            dq_copy(d, h).start()
        dq_own(h).start()
        dlat[:width, :] += latent_part
        dlat[width:, :] += rope
        k_half[...] = k_grad
        v_half[...] = v_grad
        kx_out[h] = k_half[pl.ds((1 - rep) * k_rows, k_rows), :].astype(jnp.bfloat16)
        vx_out[h] = v_half[pl.ds((1 - rep) * v_rows, v_rows), :].astype(jnp.bfloat16)
        k_copy(h).start()
        v_copy(h).start()
        dk_out[h] = k_half[pl.ds(rep * k_rows, k_rows), :]
        dv_out[h] = v_half[pl.ds(rep * v_rows, v_rows), :]
        return unused

    lax.fori_loop(0, heads, one_head, 0)

    exchange = remote(dlat.at[pl.ds((1 - sub) * half_rows, half_rows), :], half_in,
                      half_sem.at[0], half_sem.at[1], "sub", 1 - sub)
    exchange.start()

    def finish(h, unused):
        k_copy(h).wait()
        v_copy(h).wait()
        dk_out[h] += kx_in[h].astype(jnp.float32)
        dv_out[h] += vx_in[h].astype(jnp.float32)
        return unused

    exchange.wait()
    half_in[...] += dlat[pl.ds(sub * half_rows, half_rows), :]

    def columns_of(block):
        return half_in[:, pl.ds(pl.multiple_of(block * BLK, BLK), BLK)]

    piece_out[0] = columns_of(near).astype(jnp.bfloat16)
    piece_out[1] = columns_of(diagonal).astype(jnp.bfloat16)
    beside = remote(piece_out, piece_in, piece_send.at[0], piece_recv.at[0], "seq", near)
    beside.start()
    beside.wait()
    cross_out[...] = (columns_of(cross) + piece_in[1].astype(jnp.float32)).astype(jnp.bfloat16)
    over = remote(cross_out, cross_in, piece_send.at[1], piece_recv.at[1], "seq", cross)
    over.start()
    lax.fori_loop(0, heads, finish, 0)
    gathered = columns_of(me) + piece_in[0].astype(jnp.float32)
    over.wait()
    lat_out[...] = gathered + cross_in[...].astype(jnp.float32)

    def drain(h, unused):
        for d in peers:
            dq_copy(d, h).wait()
        dq_own(h).wait()
        return unused

    lax.fori_loop(0, heads, drain, 0)


def local_small(queries, grad_out, latent_kv, key_up, value_up, key_blocks, block_counts):
    shards = lax.axis_size("seq")
    heads, _, nope, width = key_up.shape
    value_width = value_up.shape[3]
    q_t = jnp.transpose(queries[0], (1, 2, 0))
    g_t = jnp.transpose(grad_out[0], (1, 0, 2))
    lat_local = latent_kv[0].T
    kv_width, tokens = lat_local.shape
    total = shards * tokens
    query_width = q_t.shape[1]
    half = kv_width // 2
    bf16, f32 = jnp.bfloat16, jnp.float32
    hbm = pl.BlockSpec(memory_space=pl.ANY)
    vmem = pl.BlockSpec(memory_space=pltpu.VMEM)
    smem = pl.BlockSpec(memory_space=pltpu.SMEM)
    sems = lambda *shape: pltpu.SemaphoreType.DMA(shape)
    far = shards - 1
    dq, dlat, dk, dv = pl.pallas_call(
        functools.partial(attention_kernel, shards, heads),
        in_specs=[smem, smem, hbm, hbm, hbm, hbm, hbm],
        out_specs=[hbm, vmem, vmem, vmem],
        out_shape=[
            jax.ShapeDtypeStruct(q_t.shape, bf16),
            jax.ShapeDtypeStruct((half, tokens), f32),
            jax.ShapeDtypeStruct((heads, nope // 2, width), f32),
            jax.ShapeDtypeStruct((heads, width // 2, value_width), f32),
        ],
        scratch_shapes=[
            pltpu.VMEM((shards, heads, query_width, tokens), bf16),
            pltpu.VMEM((shards, heads, tokens, value_width), bf16),
            pltpu.VMEM((shards, kv_width, tokens), bf16),
            pltpu.VMEM((heads, nope, width), bf16),
            pltpu.VMEM((heads, width, value_width), bf16),
            pltpu.VMEM((shards, heads, query_width, tokens), bf16),
            pltpu.VMEM((kv_width, total), bf16),
            pltpu.VMEM((total, width), bf16),
            pltpu.VMEM((total, total), f32),
            pltpu.VMEM((total, 2 * BLK), bf16),
            pltpu.VMEM((query_width, total), bf16),
            pltpu.VMEM((query_width, total), f32),
            pltpu.VMEM((total, value_width), f32),
            pltpu.VMEM((kv_width, total), f32),
            pltpu.VMEM((nope, width), f32),
            pltpu.VMEM((width, value_width), f32),
            pltpu.VMEM((heads, nope // 2, width), bf16),
            pltpu.VMEM((heads, nope // 2, width), bf16),
            pltpu.VMEM((heads, width // 2, value_width), bf16),
            pltpu.VMEM((heads, width // 2, value_width), bf16),
            pltpu.VMEM((half, total), f32),
            pltpu.VMEM((2, half, tokens), bf16),
            pltpu.VMEM((2, half, tokens), bf16),
            pltpu.VMEM((half, tokens), bf16),
            pltpu.VMEM((half, tokens), bf16),
            sems(far, heads), sems(far, heads), sems(far, heads), sems(far, heads),
            sems(far), sems(far),
            sems(far, heads), sems(far, heads), sems(heads),
            sems(2, heads), sems(2, heads), sems(2), sems(2), sems(2), sems(5),
            sems(far), sems(far),
        ],
        compiler_params=pltpu.CompilerParams(
            collective_id=0, has_side_effects=True, vmem_limit_bytes=48 << 20
        ),
    )(key_blocks[0], block_counts[0], q_t, g_t, lat_local, key_up[:, 0], value_up[:, 0])
    return (
        jnp.transpose(dq, (2, 0, 1))[None],
        dlat.T[None],
        dk[:, None],
        dv[:, None],
    )


def head_backward(
    head_queries, head_grads, latent, key_weight, value_weight, slot_list, count_list, block_rows
):
    length = head_queries.shape[0]
    latent_width = key_weight.shape[1]
    nope_width = key_weight.shape[0]
    query_width = head_queries.shape[1]
    value_width = head_grads.shape[1]
    block_count = length // block_rows
    slot_count = slot_list.shape[1]
    factor = 1.0 / math.sqrt(query_width)
    compressed = latent[:, :latent_width]
    key_nope = jnp.einsum(
        "tl,dl->td", compressed, key_weight, preferred_element_type=jnp.float32
    ).astype(jnp.bfloat16)
    values = jnp.dot(compressed, value_weight, preferred_element_type=jnp.float32).astype(
        jnp.bfloat16
    )
    keys_all = jnp.concatenate([key_nope, latent[:, latent_width:]], axis=1)
    per_group = math.gcd(block_count, max(1, 512 // block_rows))
    group_count = block_count // per_group
    key_tiles = keys_all.reshape(block_count, block_rows, query_width)
    value_tiles = values.reshape(block_count, block_rows, value_width)
    causal = lax.broadcasted_iota(jnp.int32, (block_rows, block_rows), 0) >= lax.broadcasted_iota(
        jnp.int32, (block_rows, block_rows), 1
    )
    slot_range = jnp.arange(slot_count, dtype=jnp.int32)
    within = jnp.arange(per_group, dtype=jnp.int32)

    def one_group(carry, inputs):
        key_total, value_total = carry
        query_tile, grad_tile, group_slots, group_counts, group_index = inputs
        own_blocks = group_index * per_group + within
        keys_here = key_tiles[group_slots].reshape(per_group, slot_count * block_rows, query_width)
        values_here = value_tiles[group_slots].reshape(
            per_group, slot_count * block_rows, value_width
        )
        live = slot_range[None, :] < group_counts[:, None]
        diagonal = group_slots == own_blocks[:, None]
        allowed = live[:, None, :, None] & (
            jnp.logical_not(diagonal)[:, None, :, None] | causal[None, :, None, :]
        )
        allowed = allowed.reshape(per_group, block_rows, slot_count * block_rows)
        scores = (
            jnp.einsum("gqd,gkd->gqk", query_tile, keys_here, preferred_element_type=jnp.float32)
            * factor
        )
        scores = jnp.where(allowed, scores, -1e30)
        top_score = jnp.max(scores, axis=2, keepdims=True)
        expo = jnp.where(allowed, jnp.exp(scores - top_score), 0.0)
        probs = expo / jnp.sum(expo, axis=2, keepdims=True)
        probs_b = probs.astype(jnp.bfloat16)
        attended = jnp.einsum(
            "gqk,gkd->gqd", probs_b, values_here, preferred_element_type=jnp.float32
        )
        delta = jnp.sum(grad_tile.astype(jnp.float32) * attended, axis=2, keepdims=True)
        grad_probs = jnp.einsum(
            "gqd,gkd->gqk", grad_tile, values_here, preferred_element_type=jnp.float32
        )
        grad_scores = (probs * (grad_probs - delta)).astype(jnp.bfloat16)
        grad_query = (
            jnp.einsum("gqk,gkd->gqd", grad_scores, keys_here, preferred_element_type=jnp.float32)
            * factor
        ).astype(jnp.bfloat16)
        grad_key = (
            jnp.einsum("gqk,gqd->gkd", grad_scores, query_tile, preferred_element_type=jnp.float32)
            * factor
        )
        grad_value = jnp.einsum(
            "gqk,gqd->gkd", probs_b, grad_tile, preferred_element_type=jnp.float32
        )
        flat_slots = group_slots.reshape(per_group * slot_count)
        key_total = key_total.at[flat_slots].add(
            grad_key.reshape(per_group * slot_count, block_rows, query_width)
        )
        value_total = value_total.at[flat_slots].add(
            grad_value.reshape(per_group * slot_count, block_rows, value_width)
        )
        return ((key_total, value_total), grad_query)

    start = (
        jnp.zeros((block_count, block_rows, query_width), jnp.float32),
        jnp.zeros((block_count, block_rows, value_width), jnp.float32),
    )
    inputs = (
        head_queries.reshape(group_count, per_group, block_rows, query_width),
        head_grads.reshape(group_count, per_group, block_rows, value_width),
        slot_list.reshape(group_count, per_group, slot_count),
        count_list.reshape(group_count, per_group),
        jnp.arange(group_count, dtype=jnp.int32),
    )
    (key_total, value_total), grad_tiles = lax.scan(one_group, start, inputs)
    grad_query = grad_tiles.reshape(length, query_width)
    key_grads = key_total.reshape(length, query_width)
    nope_grads = key_grads[:, :nope_width].astype(jnp.bfloat16)
    value_grads = value_total.reshape(length, value_width).astype(jnp.bfloat16)
    latent_grad = jnp.dot(nope_grads, key_weight, preferred_element_type=jnp.float32) + jnp.einsum(
        "tv,lv->tl", value_grads, value_weight, preferred_element_type=jnp.float32
    )
    head_part = jnp.concatenate([latent_grad, key_grads[:, nope_width:]], axis=1).astype(
        jnp.bfloat16
    )
    key_weight_grad = jnp.einsum(
        "td,tl->dl", nope_grads, compressed, preferred_element_type=jnp.float32
    )
    value_weight_grad = jnp.einsum(
        "tl,tv->lv", compressed, value_grads, preferred_element_type=jnp.float32
    )
    return (grad_query, head_part, key_weight_grad, value_weight_grad)


def local_general(queries, grad_out, latent_kv, key_up, value_up, key_blocks, block_counts):
    head_queries, head_grads = (
        lax.all_to_all(queries, "seq", split_axis=2, concat_axis=1, tiled=True),
        lax.all_to_all(grad_out, "seq", split_axis=2, concat_axis=1, tiled=True),
    )
    latent = lax.all_gather(latent_kv, "seq", axis=1, tiled=True)[0]
    slot_list = key_blocks[0]
    count_list = block_counts[0]
    query_stack = jnp.moveaxis(head_queries[0], 1, 0)
    grad_stack = jnp.moveaxis(head_grads[0], 1, 0)

    def one_head(carry, inputs):
        head_q, head_g, key_weight, value_weight = inputs
        results = head_backward(
            head_q, head_g, latent, key_weight, value_weight, slot_list, count_list, BLK
        )
        return (carry, results)

    unused, (query_grads, head_parts, key_grads, value_grads) = lax.scan(
        one_head,
        jnp.zeros((), jnp.float32),
        (query_stack, grad_stack, key_up[:, 0], value_up[:, 0]),
    )
    returning = jnp.moveaxis(query_grads, 0, 1)[None]
    grad_queries = lax.all_to_all(returning, "seq", split_axis=1, concat_axis=2, tiled=True)
    heads_here, length, part_width = head_parts.shape
    seq_count = lax.axis_size("seq")
    tokens_here = length // seq_count
    pieces = head_parts.reshape(heads_here, seq_count, tokens_here, part_width)
    arrived = lax.all_to_all(pieces, "seq", split_axis=1, concat_axis=1, tiled=True)
    summed = jnp.sum(arrived.astype(jnp.float32), axis=(0, 1))
    grad_latent = lax.psum_scatter(summed, "sub", scatter_dimension=1, tiled=True)
    key_grads = key_grads[:, None]
    value_grads = value_grads[:, None]
    total_key, total_value = lax.psum((key_grads, value_grads), "rep")
    replica_count = lax.axis_size("rep")
    replica_index = lax.axis_index("rep")
    key_rows = total_key.shape[2] // replica_count
    value_rows = total_value.shape[2] // replica_count
    grad_key_up = lax.dynamic_slice_in_dim(total_key, replica_index * key_rows, key_rows, 2)
    grad_value_up = lax.dynamic_slice_in_dim(total_value, replica_index * value_rows, value_rows, 2)
    return (grad_queries, grad_latent[None], grad_key_up, grad_value_up)


def solution(mesh):
    placed = (
        P(("groups", "rep"), "seq", None, "sub"),
        P(("groups", "rep"), "seq", None, "sub"),
        P(("groups", "rep"), "seq", None),
        P("seq", "sub", None, None),
        P("seq", "sub", None, None),
        P(("groups", "rep"), None, None),
        P(("groups", "rep"), None),
    )

    def local(queries, grad_out, latent_kv, key_up, value_up, key_blocks, block_counts):
        args = (queries, grad_out, latent_kv, key_up, value_up, key_blocks, block_counts)
        shards = mesh.shape["seq"]
        small = (
            queries.shape[1] == BLK
            and shards == 4
            and mesh.shape["rep"] == 2
            and mesh.shape["sub"] == 2
            and latent_kv.shape[2] % 32 == 0
        )
        return local_small(*args) if small else local_general(*args)

    return jax.shard_map(
        local,
        mesh=mesh,
        in_specs=placed,
        out_specs=(
            P(("groups", "rep"), "seq", None, "sub"),
            P(("groups", "rep"), "seq", "sub"),
            P(("groups", "seq"), "sub", "rep", None),
            P(("groups", "seq"), "sub", "rep", None),
        ),
        check_vma=False,
    )
```
